512 devices in a mesh: row: 32 (over y_hi, z), col: 16 (over x, y_lo, core).
Axes of the slice: x: 4, y: 4 (y_hi: 2, y_lo: 2; y = y_hi * 2 + y_lo), z: 16, core: 2. Of those that a mesh axis runs over, the one named last changes fastest.
Arguments:
- left_blocks: float32 [32, 32, 4, 4096], P('row', 'col'), may hold values from -0.75 to 0.75
- right_blocks: float32 [32, 16, 20, 4096], P('row', 'col'), may hold values from -6 to 6
- left_slots: int32 [32, 16, 4, 2, 24], P('row', 'col'), may hold values from 0 to 3
- right_slots: int32 [32, 16, 4, 2, 24], P('row', 'col'), may hold values from 0 to 19
- sink_slots: int32 [32, 16, 4, 2, 24], P('row', 'col'), may hold values from 0 to 11
- live_counts: int32 [32, 16, 4, 2], P('row', 'col'), may hold values from 3 to 24, as said below
Outputs:
- product_blocks: float32 [32, 16, 12, 4096], P('row', 'col')
The draws below stay inside these ranges and needn't reach their ends.
Inputs may be any that keep to these rules, and one draw needn't show every extreme that they name: `live_counts`: entries of a list at positions from its live count on are not read; at least one list in every draw is full.
All inputs are finite; a program needn't handle non-finite values.
Results may differ from the reference program's by a relative error of at most 0.0003.
Values sent between devices are 32-bit elements; how exact they have to be, the bound alone decides.
A program may use at most 64 MiB of HBM per device.

```python
import jax
import jax.numpy as jnp
from jax import lax

TILE_SIDE = 64
LEFT_SLOTS = 4
RIGHT_SLOTS = 20
SINK_SLOTS = 12
PRODUCTS = 24
SECTIONS = 4
INNER_PANELS = 32
N_ROW = 32
N_COL = 16


def draw_live_counts(key, part):
    shape = (N_ROW, N_COL, SECTIONS, 2)
    first_key, second_key, third_key = jax.random.split(key, 3)
    base_counts = jax.random.randint(first_key, shape, PRODUCTS // 8, PRODUCTS // 2 + 1)
    full_lists = jax.random.randint(second_key, shape, 0, 8) == 0
    chosen = jax.random.randint(third_key, (), 0, N_ROW * N_COL * SECTIONS * 2)
    position = jnp.arange(N_ROW * N_COL * SECTIONS * 2).reshape(shape)
    counts = jnp.where(full_lists | (position == chosen), PRODUCTS, base_counts)
    return counts.astype(jnp.int32)


def touch_ends(values, key, least, largest):
    longest = values.shape.index(max(values.shape))
    spots = []
    for shift in (0, 1):
        where = [jax.random.randint(jax.random.fold_in(key, axis), (), 0, length) for axis, length in enumerate(values.shape)]
        where[longest] = (where[longest] + shift) % values.shape[longest]
        spots.append(tuple(where))
    return values.at[spots[0]].set(least).at[spots[1]].set(largest)


def steps_of(own_key, shape, shards, least, top_value):
    gain = 1.0
    for dim, blocks in shards:
        steps = jax.random.uniform(jax.random.fold_in(jax.random.fold_in(own_key, 6), dim), (blocks,), jnp.float32, least / len(shards), top_value / len(shards))
        gain = gain * jnp.repeat(jnp.exp(steps), shape[dim] // blocks).reshape((-1,) + (1,) * (len(shape) - 1 - dim))
    return gain


def noise(stream_key, extent, deviation, limit, cuts=(), held_as=jnp.bfloat16):
    gain = steps_of(stream_key, extent, cuts, -0.22, 0.18) if cuts else 1.0
    drawn = jax.random.normal(stream_key, extent, jnp.float32) * deviation * gain
    return jnp.minimum(jnp.maximum(drawn, -limit), limit).astype(held_as)


def setup_inputs(seed: int = 0) -> dict:
    seeds = jax.random.split(jax.random.key(seed), 7)
    return {
        "left_blocks": noise(seeds[0], (N_ROW, INNER_PANELS, LEFT_SLOTS, TILE_SIDE * TILE_SIDE), TILE_SIDE ** -0.5, 0.75, ((0, 32), (1, 16)), jnp.float32),
        "right_blocks": noise(seeds[1], (INNER_PANELS, N_COL, RIGHT_SLOTS, TILE_SIDE * TILE_SIDE), 1.0, 6.0, ((0, 32), (1, 16)), jnp.float32),
        "left_slots": touch_ends(jax.random.randint(seeds[2], (N_ROW, N_COL, SECTIONS, 2, PRODUCTS), 0, LEFT_SLOTS), jax.random.fold_in(seeds[2], 1), 0, LEFT_SLOTS - 1).astype(jnp.int32),
        "right_slots": touch_ends(jax.random.randint(seeds[3], (N_ROW, N_COL, SECTIONS, 2, PRODUCTS), 0, RIGHT_SLOTS), jax.random.fold_in(seeds[3], 1), 0, RIGHT_SLOTS - 1).astype(jnp.int32),
        "sink_slots": touch_ends(jax.random.randint(seeds[4], (N_ROW, N_COL, SECTIONS, 2, PRODUCTS), 0, SINK_SLOTS), jax.random.fold_in(seeds[4], 1), 0, SINK_SLOTS - 1).astype(jnp.int32),
        "live_counts": draw_live_counts(jax.random.fold_in(seeds[6], 71), 0),
    }


def block_terms(left_panel, right_panel, left_index, right_index, sink_index, live_count):
    is_live = (jnp.arange(PRODUCTS) < live_count).astype(jnp.float32)
    left_tiles = jnp.take(left_panel, left_index, axis=0).reshape(PRODUCTS, TILE_SIDE, TILE_SIDE)
    right_tiles = jnp.take(right_panel, right_index, axis=0).reshape(PRODUCTS, TILE_SIDE, TILE_SIDE)
    products = jnp.einsum("pik,pkj->pij", left_tiles.astype(jnp.float32), right_tiles.astype(jnp.float32), precision=lax.Precision.HIGHEST)
    products = products.reshape(PRODUCTS, TILE_SIDE * TILE_SIDE) * is_live[:, None]
    return jax.ops.segment_sum(products, sink_index, num_segments=SINK_SLOTS)


def reference(left_blocks, right_blocks, left_slots, right_slots, sink_slots, live_counts):
    def one_panel(flat_index):
        row_no = flat_index // N_COL
        col_no = flat_index % N_COL
        left_row = lax.dynamic_index_in_dim(left_blocks, row_no, 0, keepdims=False)
        right_col = lax.dynamic_index_in_dim(right_blocks, col_no, 1, keepdims=False)
        running = jnp.zeros((SINK_SLOTS, TILE_SIDE * TILE_SIDE), jnp.float32)
        for section_no in range(SECTIONS):
            for half_no in range(2):
                inner = (2 * ((row_no // 2 + col_no + section_no) % N_COL) + half_no).astype(jnp.int32)
                left_panel = lax.dynamic_index_in_dim(left_row, inner, 0, keepdims=False)
                right_panel = lax.dynamic_index_in_dim(right_col, inner, 0, keepdims=False)
                running = running + block_terms(left_panel, right_panel,
                                                left_slots[row_no, col_no, section_no, half_no],
                                                right_slots[row_no, col_no, section_no, half_no],
                                                sink_slots[row_no, col_no, section_no, half_no],
                                                live_counts[row_no, col_no, section_no, half_no])
        return running

    result = lax.map(one_panel, jnp.arange(N_ROW * N_COL, dtype=jnp.int32))
    return result.reshape(N_ROW, N_COL, SINK_SLOTS, TILE_SIDE * TILE_SIDE)
```

```python
import functools

import jax
import jax.numpy as jnp
from jax import lax
from jax.experimental import pallas as pl
from jax.experimental.pallas import tpu as pltpu
from jax.sharding import PartitionSpec as P

TILE_SIDE = 64
LEFT_SLOTS = 4
RIGHT_SLOTS = 20
SINK_SLOTS = 12
PRODUCTS = 24
SECTIONS = 4
PANELS = 2 * SECTIONS
CHUNKS = 4
LEFT_ROWS = LEFT_SLOTS * TILE_SIDE
RIGHT_ROWS = RIGHT_SLOTS * TILE_SIDE // 2
CHUNK_ROWS = RIGHT_ROWS // CHUNKS
MESH = pl.DeviceIdType.MESH


def entry_offset(column):
    return column * 0 + 2


def exchange_kernel(rows, cols, left_ref, right_ref, left_all, right_all,
                    left_send, left_recv, entry_send, right_recv, down_send, up_send):
    row = lax.axis_index("row")
    column = lax.axis_index("col")
    parity = row % 2
    half_row = row // 2
    below = (row + rows - 1) % rows
    above = (row + 1) % rows
    offset = entry_offset(column)
    shift = (2 * column + offset) % rows
    entry_target = (row + rows - shift) % rows
    entry_source = (row + shift) % rows
    entry = parity + offset
    moves = shift != 0

    barrier = pltpu.get_barrier_semaphore()
    pl.semaphore_signal(barrier, inc=1, device_id=(below, column), device_id_type=MESH)
    pl.semaphore_signal(barrier, inc=1, device_id=(above, column), device_id_type=MESH)

    @pl.when(moves)
    def _():
        pl.semaphore_signal(barrier, inc=1, device_id=(entry_source, column), device_id_type=MESH)

    for section in range(SECTIONS):
        @pl.when((half_row + section) % cols != 0)
        def _():
            source = (column + half_row + section) % cols
            pl.semaphore_signal(barrier, inc=1, device_id=(row, source), device_id_type=MESH)

    peers = 2 + moves.astype(jnp.int32)
    for section in range(SECTIONS):
        peers += ((half_row + section) % cols != 0).astype(jnp.int32)
    pl.semaphore_wait(barrier, peers)

    def part(chunk):
        return pl.ds(pl.multiple_of(chunk * CHUNK_ROWS, 8), CHUNK_ROWS)

    def entry_copy(chunk):
        return pltpu.make_async_remote_copy(
            src_ref=right_ref.at[part(chunk)], dst_ref=right_all.at[entry, part(chunk)],
            send_sem=entry_send.at[chunk], recv_sem=right_recv.at[entry, chunk],
            device_id=(entry_target, column), device_id_type=MESH)

    def local_copy(chunk):
        return pltpu.make_async_copy(
            right_ref.at[part(chunk)], right_all.at[entry, part(chunk)], right_recv.at[entry, chunk])

    def left_copy(section):
        target = (column + 2 * cols - half_row - section) % cols
        return pltpu.make_async_remote_copy(
            src_ref=left_ref, dst_ref=left_all.at[section],
            send_sem=left_send.at[section], recv_sem=left_recv.at[section],
            device_id=(row, target), device_id_type=MESH)

    def left_local(section):
        return pltpu.make_async_copy(left_ref, left_all.at[section], left_recv.at[section])

    def down_copy(slot, chunk):
        return pltpu.make_async_remote_copy(
            src_ref=right_all.at[slot, part(chunk)],
            dst_ref=right_all.at[slot + 2 * (1 - parity), part(chunk)],
            send_sem=down_send.at[slot, chunk],
            recv_sem=right_recv.at[slot + 2 * (1 - parity), chunk],
            device_id=(below, column), device_id_type=MESH)

    def up_copy(slot, chunk):
        return pltpu.make_async_remote_copy(
            src_ref=right_all.at[slot, part(chunk)],
            dst_ref=right_all.at[slot - 2 * parity, part(chunk)],
            send_sem=up_send.at[slot, chunk],
            recv_sem=right_recv.at[slot - 2 * parity, chunk],
            device_id=(above, column), device_id_type=MESH)

    for chunk in range(CHUNKS):
        @pl.when(moves)
        def _():
            entry_copy(chunk).start()

        @pl.when(jnp.logical_not(moves))
        def _():
            local_copy(chunk).start()

    for section in range(SECTIONS):
        @pl.when((half_row + section) % cols != 0)
        def _():
            left_copy(section).start()

        @pl.when((half_row + section) % cols == 0)
        def _():
            left_local(section).start()

    last_down = PANELS - 1 - 2 * (1 - parity)
    last_up = 2 * parity

    def arrived(slot, chunk):
        pltpu.make_async_copy(
            right_ref.at[part(chunk)], right_all.at[slot, part(chunk)], right_recv.at[slot, chunk]).wait()

    def first(chunk, carry):
        arrived(entry, chunk)

        @pl.when(entry <= last_down)
        def _():
            down_copy(entry, chunk).start()

        @pl.when(entry >= last_up)
        def _():
            up_copy(entry, chunk).start()
        return carry

    lax.fori_loop(0, CHUNKS, first, 0)

    def onward(step, carry):
        distance = step // CHUNKS + 1
        chunk = step % CHUNKS
        higher = entry + distance
        lower = entry - distance

        @pl.when(higher < PANELS)
        def _():
            arrived(higher, chunk)

        @pl.when(higher <= last_down)
        def _():
            down_copy(higher, chunk).start()

        @pl.when(lower >= 0)
        def _():
            arrived(lower, chunk)

        @pl.when(lower >= last_up)
        def _():
            up_copy(lower, chunk).start()
        return carry

    lax.fori_loop(0, (PANELS - 1) * CHUNKS, onward, 0)

    def sent(step, carry):
        slot = step // CHUNKS
        chunk = step % CHUNKS

        @pl.when((slot >= entry) & (slot <= last_down))
        def _():
            down_copy(slot, chunk).wait_send()

        @pl.when((slot <= entry) & (slot >= last_up))
        def _():
            up_copy(slot, chunk).wait_send()
        return carry

    lax.fori_loop(0, PANELS * CHUNKS, sent, 0)

    for chunk in range(CHUNKS):
        @pl.when(moves)
        def _():
            entry_copy(chunk).wait_send()

    for section in range(SECTIONS):
        @pl.when((half_row + section) % cols != 0)
        def _():
            left_copy(section).wait()

        @pl.when((half_row + section) % cols == 0)
        def _():
            left_local(section).wait()


def exchange(rows, cols, left, right):
    dma = pltpu.SemaphoreType.DMA
    return pl.pallas_call(
        functools.partial(exchange_kernel, rows, cols),
        out_shape=(
            jax.ShapeDtypeStruct((SECTIONS, LEFT_ROWS, 2 * TILE_SIDE), jnp.float32),
            jax.ShapeDtypeStruct((PANELS, RIGHT_ROWS, 2 * TILE_SIDE), jnp.float32),
        ),
        in_specs=[pl.BlockSpec(memory_space=pltpu.VMEM)] * 2,
        out_specs=(pl.BlockSpec(memory_space=pltpu.VMEM),) * 2,
        scratch_shapes=[
            dma((SECTIONS,)), dma((SECTIONS,)), dma((CHUNKS,)), dma((PANELS, CHUNKS)),
            dma((PANELS, CHUNKS)), dma((PANELS, CHUNKS)),
        ],
        compiler_params=pltpu.CompilerParams(collective_id=0, has_side_effects=True),
        name="exchange",
    )(left, right)


def product_kernel(left_lists, right_lists, sink_lists, counts, left_all, right_all, out, products, sums):
    side = TILE_SIDE
    sums[...] = jnp.zeros_like(sums)
    lane = lax.broadcasted_iota(jnp.int32, (LEFT_ROWS, 2 * side), 1)

    def section_body(section, carry):
        left = left_all[section]
        turned = pltpu.roll(left, side, 1)
        for half in range(2):
            own, other = (left, turned) if half == 0 else (turned, left)
            twice = jnp.where(lane < side, own, other)
            high = twice.astype(jnp.bfloat16).astype(jnp.float32)
            split = jnp.where(lane < side, high, twice - high).astype(jnp.bfloat16)
            stream = jnp.concatenate([split, split], axis=1)
            item = 2 * section + half
            for quad in range(RIGHT_SLOTS // 4):
                right = jnp.concatenate(
                    [right_all[item, pl.ds((2 * quad + n) * side, side), :] for n in range(2)], axis=1)
                right_high = right.astype(jnp.bfloat16)
                right_low = (right - right_high.astype(jnp.float32)).astype(jnp.bfloat16)
                held = jnp.concatenate([right_high, right_high, right_low, right_low], axis=0)
                found = jnp.dot(stream, held, preferred_element_type=jnp.float32)
                for n in range(2):
                    products[pl.ds(LEFT_SLOTS * (2 * quad + n), LEFT_SLOTS)] = (
                        found[:, 2 * side * n : 2 * side * (n + 1)].reshape(LEFT_SLOTS, side, 2 * side))

            def add(position, inner):
                right_slot = right_lists[item, position]
                source = LEFT_SLOTS * (right_slot >> 1) + left_lists[item, position]
                sink = 2 * sink_lists[item, position] + (right_slot & 1)
                sums[sink] += products[source]
                return inner

            lax.fori_loop(0, counts[item], add, 0)
        return carry

    lax.fori_loop(0, SECTIONS, section_body, 0)
    for sink in range(SINK_SLOTS):
        total = sums[2 * sink] + pltpu.roll(sums[2 * sink + 1], side, 1)
        out[sink] = total[:, :side]


def product_sums(left_lists, right_lists, sink_lists, counts, left_all, right_all):
    smem = pl.BlockSpec(memory_space=pltpu.SMEM)
    vmem = pl.BlockSpec(memory_space=pltpu.VMEM)
    return pl.pallas_call(
        product_kernel,
        out_shape=jax.ShapeDtypeStruct((SINK_SLOTS, TILE_SIDE, TILE_SIDE), jnp.float32),
        in_specs=[smem] * 4 + [vmem] * 2,
        out_specs=vmem,
        scratch_shapes=[
            pltpu.VMEM((LEFT_SLOTS * RIGHT_SLOTS // 2, TILE_SIDE, 2 * TILE_SIDE), jnp.float32),
            pltpu.VMEM((2 * SINK_SLOTS, TILE_SIDE, 2 * TILE_SIDE), jnp.float32),
        ],
        name="product_sums",
    )(left_lists, right_lists, sink_lists, counts, left_all, right_all)


def per_device(rows, cols, left_blocks, right_blocks, left_slots, right_slots, sink_slots, live_counts):
    side = TILE_SIDE
    right = right_blocks.reshape(RIGHT_SLOTS // 2, 2, side, side).transpose(0, 2, 1, 3).reshape(RIGHT_ROWS, 2 * side)
    left = left_blocks.reshape(2, LEFT_ROWS, side).transpose(1, 0, 2).reshape(LEFT_ROWS, 2 * side)
    left_all, right_all = exchange(rows, cols, left, right)
    total = product_sums(
        left_slots.reshape(PANELS, PRODUCTS), right_slots.reshape(PANELS, PRODUCTS),
        sink_slots.reshape(PANELS, PRODUCTS), live_counts.reshape(PANELS), left_all, right_all)
    return total.reshape(1, 1, SINK_SLOTS, side * side)


def solution(mesh):
    return jax.shard_map(
        functools.partial(per_device, mesh.shape["row"], mesh.shape["col"]),
        mesh=mesh,
        in_specs=(
            P("row", "col", None, None),
            P("row", "col", None, None),
            P("row", "col", None, None, None),
            P("row", "col", None, None, None),
            P("row", "col", None, None, None),
            P("row", "col", None, None),
        ),
        out_specs=P("row", "col", None, None),
        check_vma=False,
    )
```

```python
import functools

import jax
import jax.numpy as jnp
from jax import lax
from jax.experimental import pallas as pl
from jax.experimental.pallas import tpu as pltpu
from jax.sharding import PartitionSpec as P

TILE_SIDE = 64
LEFT_SLOTS = 4
RIGHT_SLOTS = 20
SINK_SLOTS = 12
PRODUCTS = 24
SECTIONS = 4
PANELS = 2 * SECTIONS
CHUNKS = 4
LEFT_ROWS = LEFT_SLOTS * TILE_SIDE
RIGHT_ROWS = RIGHT_SLOTS * TILE_SIDE // 2
CHUNK_ROWS = RIGHT_ROWS // CHUNKS
TURNED = CHUNKS // 2
MESH = pl.DeviceIdType.MESH


def chosen(column, values):
    total = 0
    for place, value in enumerate(values):
        if value:
            total = total + (column % len(values) == place).astype(jnp.int32) * value
    return total


def exchange_kernel(rows, cols, left_ref, right_ref, left_all, right_all, relay,
                    left_send, left_recv, entry_send, right_recv, down_send, up_send,
                    relay_send, relay_recv):
    row = lax.axis_index("row")
    column = lax.axis_index("col")
    parity = row % 2
    half_row = row // 2
    below = (row + rows - 1) % rows
    above = (row + 1) % rows
    offset = chosen(column, (0, 0, 0, 6, 6, 6, 4, 2))
    turned_offset = chosen(column, (0, 6, 0, 6, 0, 6, 4, 2))
    relay_shift = chosen(column, (0, rows - 4, 0, 0, 4, 0, 0, 0))
    relays = relay_shift != 0
    shift = (2 * column + offset) % rows
    final_shift = (2 * column + turned_offset + rows - relay_shift) % rows
    moves = shift != 0
    greets_final = relays & (final_shift != relay_shift)

    def greet(row_to, column_to):
        pl.semaphore_signal(barrier, inc=1, device_id=(row_to, column_to), device_id_type=MESH)

    barrier = pltpu.get_barrier_semaphore()
    greet(below, column)
    greet(above, column)

    @pl.when(moves)
    def _():
        greet((row + shift) % rows, column)

    @pl.when(relays)
    def _():
        greet((row + relay_shift) % rows, column)

    @pl.when(greets_final)
    def _():
        greet((row + final_shift) % rows, column)

    for section in range(SECTIONS):
        @pl.when((half_row + section) % cols != 0)
        def _():
            greet(row, (column + half_row + section) % cols)

    peers = 2 + moves.astype(jnp.int32) + relays.astype(jnp.int32) + greets_final.astype(jnp.int32)
    for section in range(SECTIONS):
        peers += ((half_row + section) % cols != 0).astype(jnp.int32)
    pl.semaphore_wait(barrier, peers)

    def entry_of(chunk):
        if isinstance(chunk, int):
            return parity + (turned_offset if chunk < TURNED else offset)
        return parity + offset + (chunk < TURNED).astype(jnp.int32) * (turned_offset - offset)

    def part(chunk):
        return pl.ds(pl.multiple_of(chunk * CHUNK_ROWS, 8), CHUNK_ROWS)

    def entry_copy(chunk):
        return pltpu.make_async_remote_copy(
            src_ref=right_ref.at[part(chunk)], dst_ref=right_all.at[entry_of(chunk), part(chunk)],
            send_sem=entry_send.at[chunk], recv_sem=right_recv.at[entry_of(chunk), chunk],
            device_id=((row + rows - shift) % rows, column), device_id_type=MESH)

    def local_copy(chunk):
        return pltpu.make_async_copy(
            right_ref.at[part(chunk)], right_all.at[entry_of(chunk), part(chunk)],
            right_recv.at[entry_of(chunk), chunk])

    def relay_copy(chunk):
        return pltpu.make_async_remote_copy(
            src_ref=right_ref.at[part(chunk)], dst_ref=relay.at[part(chunk)],
            send_sem=entry_send.at[chunk], recv_sem=relay_recv.at[chunk],
            device_id=((row + rows - relay_shift) % rows, column), device_id_type=MESH)

    def final_copy(chunk):
        return pltpu.make_async_remote_copy(
            src_ref=relay.at[part(chunk)], dst_ref=right_all.at[entry_of(chunk), part(chunk)],
            send_sem=relay_send.at[chunk], recv_sem=right_recv.at[entry_of(chunk), chunk],
            device_id=((row + rows - final_shift) % rows, column), device_id_type=MESH)

    def left_copy(section):
        target = (column + 2 * cols - half_row - section) % cols
        return pltpu.make_async_remote_copy(
            src_ref=left_ref, dst_ref=left_all.at[section],
            send_sem=left_send.at[section], recv_sem=left_recv.at[section],
            device_id=(row, target), device_id_type=MESH)

    def left_local(section):
        return pltpu.make_async_copy(left_ref, left_all.at[section], left_recv.at[section])

    def down_copy(slot, chunk):
        return pltpu.make_async_remote_copy(
            src_ref=right_all.at[slot, part(chunk)],
            dst_ref=right_all.at[slot + 2 * (1 - parity), part(chunk)],
            send_sem=down_send.at[slot, chunk],
            recv_sem=right_recv.at[slot + 2 * (1 - parity), chunk],
            device_id=(below, column), device_id_type=MESH)

    def up_copy(slot, chunk):
        return pltpu.make_async_remote_copy(
            src_ref=right_all.at[slot, part(chunk)],
            dst_ref=right_all.at[slot - 2 * parity, part(chunk)],
            send_sem=up_send.at[slot, chunk],
            recv_sem=right_recv.at[slot - 2 * parity, chunk],
            device_id=(above, column), device_id_type=MESH)

    for chunk in range(CHUNKS):
        direct = moves if chunk >= TURNED else moves & jnp.logical_not(relays)

        @pl.when(direct)
        def _():
            entry_copy(chunk).start()

        @pl.when(jnp.logical_not(moves))
        def _():
            local_copy(chunk).start()

        if chunk < TURNED:
            @pl.when(relays)
            def _():
                relay_copy(chunk).start()

    for section in range(SECTIONS):
        @pl.when((half_row + section) % cols != 0)
        def _():
            left_copy(section).start()

        @pl.when((half_row + section) % cols == 0)
        def _():
            left_local(section).start()

    last_down = PANELS - 1 - 2 * (1 - parity)
    last_up = 2 * parity

    def arrived(slot, chunk):
        pltpu.make_async_copy(
            right_ref.at[part(chunk)], right_all.at[slot, part(chunk)], right_recv.at[slot, chunk]).wait()

    def first(chunk, carry):
        entry = entry_of(chunk)
        arrived(entry, chunk)

        @pl.when(entry <= last_down)
        def _():
            down_copy(entry, chunk).start()

        @pl.when(entry >= last_up)
        def _():
            up_copy(entry, chunk).start()
        return carry

    lax.fori_loop(TURNED, CHUNKS, first, 0)

    @pl.when(relays)
    def _():
        for chunk in range(TURNED):
            relay_copy(chunk).wait_recv()
            final_copy(chunk).start()

    lax.fori_loop(0, TURNED, first, 0)

    def onward(step, carry):
        distance = step // CHUNKS + 1
        chunk = (step + TURNED) % CHUNKS
        higher = entry_of(chunk) + distance
        lower = entry_of(chunk) - distance

        @pl.when(higher < PANELS)
        def _():
            arrived(higher, chunk)

        @pl.when(higher <= last_down)
        def _():
            down_copy(higher, chunk).start()

        @pl.when(lower >= 0)
        def _():
            arrived(lower, chunk)

        @pl.when(lower >= last_up)
        def _():
            up_copy(lower, chunk).start()
        return carry

    lax.fori_loop(0, (PANELS - 1) * CHUNKS, onward, 0)

    def sent(step, carry):
        slot = step // CHUNKS
        chunk = step % CHUNKS
        entry = entry_of(chunk)

        @pl.when((slot >= entry) & (slot <= last_down))
        def _():
            down_copy(slot, chunk).wait_send()

        @pl.when((slot <= entry) & (slot >= last_up))
        def _():
            up_copy(slot, chunk).wait_send()
        return carry

    lax.fori_loop(0, PANELS * CHUNKS, sent, 0)

    for chunk in range(CHUNKS):
        @pl.when(moves)
        def _():
            entry_copy(chunk).wait_send()

        if chunk < TURNED:
            @pl.when(relays)
            def _():
                final_copy(chunk).wait_send()

    for section in range(SECTIONS):
        @pl.when((half_row + section) % cols != 0)
        def _():
            left_copy(section).wait()

        @pl.when((half_row + section) % cols == 0)
        def _():
            left_local(section).wait()


def exchange(rows, cols, left, right):
    dma = pltpu.SemaphoreType.DMA
    return pl.pallas_call(
        functools.partial(exchange_kernel, rows, cols),
        out_shape=(
            jax.ShapeDtypeStruct((SECTIONS, LEFT_ROWS, 2 * TILE_SIDE), jnp.float32),
            jax.ShapeDtypeStruct((PANELS, RIGHT_ROWS, 2 * TILE_SIDE), jnp.float32),
        ),
        in_specs=[pl.BlockSpec(memory_space=pltpu.VMEM)] * 2,
        out_specs=(pl.BlockSpec(memory_space=pltpu.VMEM),) * 2,
        scratch_shapes=[
            pltpu.VMEM((TURNED * CHUNK_ROWS, 2 * TILE_SIDE), jnp.float32),
            dma((SECTIONS,)), dma((SECTIONS,)), dma((CHUNKS,)), dma((PANELS, CHUNKS)),
            dma((PANELS, CHUNKS)), dma((PANELS, CHUNKS)), dma((TURNED,)), dma((TURNED,)),
        ],
        compiler_params=pltpu.CompilerParams(collective_id=0, has_side_effects=True),
        name="exchange",
    )(left, right)


def product_kernel(left_lists, right_lists, sink_lists, counts, left_all, right_all, out, products, sums):
    side = TILE_SIDE
    sums[...] = jnp.zeros_like(sums)
    lane = lax.broadcasted_iota(jnp.int32, (LEFT_ROWS, 2 * side), 1)

    def section_body(section, carry):
        left = left_all[section]
        turned = pltpu.roll(left, side, 1)
        for half in range(2):
            own, other = (left, turned) if half == 0 else (turned, left)
            twice = jnp.where(lane < side, own, other)
            high = twice.astype(jnp.bfloat16).astype(jnp.float32)
            split = jnp.where(lane < side, high, twice - high).astype(jnp.bfloat16)
            stream = jnp.concatenate([split, split], axis=1)
            item = 2 * section + half
            for quad in range(RIGHT_SLOTS // 4):
                right = jnp.concatenate(
                    [right_all[item, pl.ds((2 * quad + n) * side, side), :] for n in range(2)], axis=1)
                right_high = right.astype(jnp.bfloat16)
                right_low = (right - right_high.astype(jnp.float32)).astype(jnp.bfloat16)
                held = jnp.concatenate([right_high, right_high, right_low, right_low], axis=0)
                found = jnp.dot(stream, held, preferred_element_type=jnp.float32)
                for n in range(2):
                    products[pl.ds(LEFT_SLOTS * (2 * quad + n), LEFT_SLOTS)] = (
                        found[:, 2 * side * n : 2 * side * (n + 1)].reshape(LEFT_SLOTS, side, 2 * side))

            def add(position, inner):
                right_slot = right_lists[item, position]
                source = LEFT_SLOTS * (right_slot >> 1) + left_lists[item, position]
                sink = 2 * sink_lists[item, position] + (right_slot & 1)
                sums[sink] += products[source]
                return inner

            lax.fori_loop(0, counts[item], add, 0)
        return carry

    lax.fori_loop(0, SECTIONS, section_body, 0)
    for sink in range(SINK_SLOTS):
        total = sums[2 * sink] + pltpu.roll(sums[2 * sink + 1], side, 1)
        out[sink] = total[:, :side]


def product_sums(left_lists, right_lists, sink_lists, counts, left_all, right_all):
    smem = pl.BlockSpec(memory_space=pltpu.SMEM)
    vmem = pl.BlockSpec(memory_space=pltpu.VMEM)
    return pl.pallas_call(
        product_kernel,
        out_shape=jax.ShapeDtypeStruct((SINK_SLOTS, TILE_SIDE, TILE_SIDE), jnp.float32),
        in_specs=[smem] * 4 + [vmem] * 2,
        out_specs=vmem,
        scratch_shapes=[
            pltpu.VMEM((LEFT_SLOTS * RIGHT_SLOTS // 2, TILE_SIDE, 2 * TILE_SIDE), jnp.float32),
            pltpu.VMEM((2 * SINK_SLOTS, TILE_SIDE, 2 * TILE_SIDE), jnp.float32),
        ],
        name="product_sums",
    )(left_lists, right_lists, sink_lists, counts, left_all, right_all)


def per_device(rows, cols, left_blocks, right_blocks, left_slots, right_slots, sink_slots, live_counts):
    side = TILE_SIDE
    right = right_blocks.reshape(RIGHT_SLOTS // 2, 2, side, side).transpose(0, 2, 1, 3).reshape(RIGHT_ROWS, 2 * side)
    left = left_blocks.reshape(2, LEFT_ROWS, side).transpose(1, 0, 2).reshape(LEFT_ROWS, 2 * side)
    left_all, right_all = exchange(rows, cols, left, right)
    total = product_sums(
        left_slots.reshape(PANELS, PRODUCTS), right_slots.reshape(PANELS, PRODUCTS),
        sink_slots.reshape(PANELS, PRODUCTS), live_counts.reshape(PANELS), left_all, right_all)
    return total.reshape(1, 1, SINK_SLOTS, side * side)


def solution(mesh):
    return jax.shard_map(
        functools.partial(per_device, mesh.shape["row"], mesh.shape["col"]),
        mesh=mesh,
        in_specs=(
            P("row", "col", None, None),
            P("row", "col", None, None),
            P("row", "col", None, None, None),
            P("row", "col", None, None, None),
            P("row", "col", None, None, None),
            P("row", "col", None, None),
        ),
        out_specs=P("row", "col", None, None),
        check_vma=False,
    )
```

```python
import functools

import jax
import jax.numpy as jnp
from jax import lax
from jax.experimental import pallas as pl
from jax.experimental.pallas import tpu as pltpu
from jax.sharding import PartitionSpec as P

TILE_SIDE = 64
LEFT_SLOTS = 4
RIGHT_SLOTS = 20
SINK_SLOTS = 12
PRODUCTS = 24
SECTIONS = 4
PANELS = 2 * SECTIONS
CHUNKS = 8
LEFT_ROWS = LEFT_SLOTS * TILE_SIDE
RIGHT_ROWS = RIGHT_SLOTS * TILE_SIDE // 2
CHUNK_ROWS = RIGHT_ROWS // CHUNKS
TURNED = 5
LAG = 2
MESH = pl.DeviceIdType.MESH


def chosen(column, values):
    total = 0
    for place, value in enumerate(values):
        if value:
            total = total + (column % len(values) == place).astype(jnp.int32) * value
    return total


def exchange_kernel(rows, cols, left_ref, right_ref, left_all, right_all, relay,
                    left_send, left_recv, entry_send, right_recv, down_send, up_send,
                    relay_send, relay_recv):
    row = lax.axis_index("row")
    column = lax.axis_index("col")
    parity = row % 2
    half_row = row // 2
    below = (row + rows - 1) % rows
    above = (row + 1) % rows
    offset = chosen(column, (0, 0, 0, 6, 6, 6, 4, 2))
    turned_offset = chosen(column, (0, 6, 0, 6, 0, 6, 4, 2))
    relay_shift = chosen(column, (0, rows - 4, 0, 0, 4, 0, 0, 0))
    relays = relay_shift != 0
    shift = (2 * column + offset) % rows
    final_shift = (2 * column + turned_offset + rows - relay_shift) % rows
    moves = shift != 0
    greets_final = relays & (final_shift != relay_shift)

    def greet(row_to, column_to):
        pl.semaphore_signal(barrier, inc=1, device_id=(row_to, column_to), device_id_type=MESH)

    barrier = pltpu.get_barrier_semaphore()
    greet(below, column)
    greet(above, column)

    @pl.when(moves)
    def _():
        greet((row + shift) % rows, column)

    @pl.when(relays)
    def _():
        greet((row + relay_shift) % rows, column)

    @pl.when(greets_final)
    def _():
        greet((row + final_shift) % rows, column)

    for section in range(SECTIONS):
        @pl.when((half_row + section) % cols != 0)
        def _():
            greet(row, (column + half_row + section) % cols)

    peers = 2 + moves.astype(jnp.int32) + relays.astype(jnp.int32) + greets_final.astype(jnp.int32)
    for section in range(SECTIONS):
        peers += ((half_row + section) % cols != 0).astype(jnp.int32)
    pl.semaphore_wait(barrier, peers)

    def entry_of(chunk):
        if isinstance(chunk, int):
            return parity + (turned_offset if chunk < TURNED else offset)
        return parity + offset + (chunk < TURNED).astype(jnp.int32) * (turned_offset - offset)

    def part(chunk):
        return pl.ds(pl.multiple_of(chunk * CHUNK_ROWS, 8), CHUNK_ROWS)

    def entry_copy(chunk):
        return pltpu.make_async_remote_copy(
            src_ref=right_ref.at[part(chunk)], dst_ref=right_all.at[entry_of(chunk), part(chunk)],
            send_sem=entry_send.at[chunk], recv_sem=right_recv.at[entry_of(chunk), chunk],
            device_id=((row + rows - shift) % rows, column), device_id_type=MESH)

    def local_copy(chunk):
        return pltpu.make_async_copy(
            right_ref.at[part(chunk)], right_all.at[entry_of(chunk), part(chunk)],
            right_recv.at[entry_of(chunk), chunk])

    def relay_copy(chunk):
        return pltpu.make_async_remote_copy(
            src_ref=right_ref.at[part(chunk)], dst_ref=relay.at[part(chunk)],
            send_sem=entry_send.at[chunk], recv_sem=relay_recv.at[chunk],
            device_id=((row + rows - relay_shift) % rows, column), device_id_type=MESH)

    def final_copy(chunk):
        return pltpu.make_async_remote_copy(
            src_ref=relay.at[part(chunk)], dst_ref=right_all.at[entry_of(chunk), part(chunk)],
            send_sem=relay_send.at[chunk], recv_sem=right_recv.at[entry_of(chunk), chunk],
            device_id=((row + rows - final_shift) % rows, column), device_id_type=MESH)

    def left_copy(section):
        target = (column + 2 * cols - half_row - section) % cols
        return pltpu.make_async_remote_copy(
            src_ref=left_ref, dst_ref=left_all.at[section],
            send_sem=left_send.at[section], recv_sem=left_recv.at[section],
            device_id=(row, target), device_id_type=MESH)

    def left_local(section):
        return pltpu.make_async_copy(left_ref, left_all.at[section], left_recv.at[section])

    def down_copy(slot, chunk):
        return pltpu.make_async_remote_copy(
            src_ref=right_all.at[slot, part(chunk)],
            dst_ref=right_all.at[slot + 2 * (1 - parity), part(chunk)],
            send_sem=down_send.at[slot, chunk],
            recv_sem=right_recv.at[slot + 2 * (1 - parity), chunk],
            device_id=(below, column), device_id_type=MESH)

    def up_copy(slot, chunk):
        return pltpu.make_async_remote_copy(
            src_ref=right_all.at[slot, part(chunk)],
            dst_ref=right_all.at[slot - 2 * parity, part(chunk)],
            send_sem=up_send.at[slot, chunk],
            recv_sem=right_recv.at[slot - 2 * parity, chunk],
            device_id=(above, column), device_id_type=MESH)

    for chunk in range(CHUNKS):
        direct = moves if chunk >= TURNED else moves & jnp.logical_not(relays)

        @pl.when(direct)
        def _():
            entry_copy(chunk).start()

        @pl.when(jnp.logical_not(moves))
        def _():
            local_copy(chunk).start()

        if chunk < TURNED:
            @pl.when(relays)
            def _():
                relay_copy(chunk).start()

    for section in range(SECTIONS):
        @pl.when((half_row + section) % cols != 0)
        def _():
            left_copy(section).start()

        @pl.when((half_row + section) % cols == 0)
        def _():
            left_local(section).start()

    last_down = PANELS - 1 - 2 * (1 - parity)
    last_up = 2 * parity

    def arrived(slot, chunk):
        pltpu.make_async_copy(
            right_ref.at[part(chunk)], right_all.at[slot, part(chunk)], right_recv.at[slot, chunk]).wait()

    def first(chunk, carry):
        entry = entry_of(chunk)
        arrived(entry, chunk)

        @pl.when(entry <= last_down)
        def _():
            down_copy(entry, chunk).start()

        @pl.when(entry >= last_up)
        def _():
            up_copy(entry, chunk).start()
        return carry

    lax.fori_loop(TURNED, CHUNKS, first, 0)

    @pl.when(relays)
    def _():
        for chunk in range(TURNED):
            relay_copy(chunk).wait_recv()
            final_copy(chunk).start()

    lag = LAG * relays.astype(jnp.int32)

    def onward(step, carry):
        chunk = (step + TURNED) % CHUNKS
        turned = chunk < TURNED
        distance = step // CHUNKS - lag * turned.astype(jnp.int32)
        begun = (distance > 0) | (turned & (distance == 0))
        higher = entry_of(chunk) + distance
        lower = entry_of(chunk) - distance

        @pl.when(begun & (higher < PANELS))
        def _():
            arrived(higher, chunk)

        @pl.when(begun & (higher <= last_down))
        def _():
            down_copy(higher, chunk).start()

        @pl.when((distance > 0) & (lower >= 0))
        def _():
            arrived(lower, chunk)

        @pl.when(begun & (lower >= last_up))
        def _():
            up_copy(lower, chunk).start()
        return carry

    lax.fori_loop(0, (PANELS + LAG) * CHUNKS, onward, 0)

    def sent(step, carry):
        slot = step // CHUNKS
        chunk = step % CHUNKS
        entry = entry_of(chunk)

        @pl.when((slot >= entry) & (slot <= last_down))
        def _():
            down_copy(slot, chunk).wait_send()

        @pl.when((slot <= entry) & (slot >= last_up))
        def _():
            up_copy(slot, chunk).wait_send()
        return carry

    lax.fori_loop(0, PANELS * CHUNKS, sent, 0)

    for chunk in range(CHUNKS):
        @pl.when(moves)
        def _():
            entry_copy(chunk).wait_send()

        if chunk < TURNED:
            @pl.when(relays)
            def _():
                final_copy(chunk).wait_send()

    for section in range(SECTIONS):
        @pl.when((half_row + section) % cols != 0)
        def _():
            left_copy(section).wait()

        @pl.when((half_row + section) % cols == 0)
        def _():
            left_local(section).wait()


def exchange(rows, cols, left, right):
    dma = pltpu.SemaphoreType.DMA
    return pl.pallas_call(
        functools.partial(exchange_kernel, rows, cols),
        out_shape=(
            jax.ShapeDtypeStruct((SECTIONS, LEFT_ROWS, 2 * TILE_SIDE), jnp.float32),
            jax.ShapeDtypeStruct((PANELS, RIGHT_ROWS, 2 * TILE_SIDE), jnp.float32),
        ),
        in_specs=[pl.BlockSpec(memory_space=pltpu.VMEM)] * 2,
        out_specs=(pl.BlockSpec(memory_space=pltpu.VMEM),) * 2,
        scratch_shapes=[
            pltpu.VMEM((TURNED * CHUNK_ROWS, 2 * TILE_SIDE), jnp.float32),
            dma((SECTIONS,)), dma((SECTIONS,)), dma((CHUNKS,)), dma((PANELS, CHUNKS)),
            dma((PANELS, CHUNKS)), dma((PANELS, CHUNKS)), dma((TURNED,)), dma((TURNED,)),
        ],
        compiler_params=pltpu.CompilerParams(collective_id=0, has_side_effects=True),
        name="exchange",
    )(left, right)


def product_kernel(left_lists, right_lists, sink_lists, counts, left_all, right_all, out, products, sums):
    side = TILE_SIDE
    sums[...] = jnp.zeros_like(sums)
    lane = lax.broadcasted_iota(jnp.int32, (LEFT_ROWS, 2 * side), 1)

    def section_body(section, carry):
        left = left_all[section]
        turned = pltpu.roll(left, side, 1)
        for half in range(2):
            own, other = (left, turned) if half == 0 else (turned, left)
            twice = jnp.where(lane < side, own, other)
            high = twice.astype(jnp.bfloat16).astype(jnp.float32)
            split = jnp.where(lane < side, high, twice - high).astype(jnp.bfloat16)
            stream = jnp.concatenate([split, split], axis=1)
            item = 2 * section + half
            for quad in range(RIGHT_SLOTS // 4):
                right = jnp.concatenate(
                    [right_all[item, pl.ds((2 * quad + n) * side, side), :] for n in range(2)], axis=1)
                right_high = right.astype(jnp.bfloat16)
                right_low = (right - right_high.astype(jnp.float32)).astype(jnp.bfloat16)
                held = jnp.concatenate([right_high, right_high, right_low, right_low], axis=0)
                found = jnp.dot(stream, held, preferred_element_type=jnp.float32)
                for n in range(2):
                    products[pl.ds(LEFT_SLOTS * (2 * quad + n), LEFT_SLOTS)] = (
                        found[:, 2 * side * n : 2 * side * (n + 1)].reshape(LEFT_SLOTS, side, 2 * side))

            def add(position, inner):
                right_slot = right_lists[item, position]
                source = LEFT_SLOTS * (right_slot >> 1) + left_lists[item, position]
                sink = 2 * sink_lists[item, position] + (right_slot & 1)
                sums[sink] += products[source]
                return inner

            lax.fori_loop(0, counts[item], add, 0)
        return carry

    lax.fori_loop(0, SECTIONS, section_body, 0)
    for sink in range(SINK_SLOTS):
        total = sums[2 * sink] + pltpu.roll(sums[2 * sink + 1], side, 1)
        out[sink] = total[:, :side]


def product_sums(left_lists, right_lists, sink_lists, counts, left_all, right_all):
    smem = pl.BlockSpec(memory_space=pltpu.SMEM)
    vmem = pl.BlockSpec(memory_space=pltpu.VMEM)
    return pl.pallas_call(
        product_kernel,
        out_shape=jax.ShapeDtypeStruct((SINK_SLOTS, TILE_SIDE, TILE_SIDE), jnp.float32),
        in_specs=[smem] * 4 + [vmem] * 2,
        out_specs=vmem,
        scratch_shapes=[
            pltpu.VMEM((LEFT_SLOTS * RIGHT_SLOTS // 2, TILE_SIDE, 2 * TILE_SIDE), jnp.float32),
            pltpu.VMEM((2 * SINK_SLOTS, TILE_SIDE, 2 * TILE_SIDE), jnp.float32),
        ],
        name="product_sums",
    )(left_lists, right_lists, sink_lists, counts, left_all, right_all)


def per_device(rows, cols, left_blocks, right_blocks, left_slots, right_slots, sink_slots, live_counts):
    side = TILE_SIDE
    right = right_blocks.reshape(RIGHT_SLOTS // 2, 2, side, side).transpose(0, 2, 1, 3).reshape(RIGHT_ROWS, 2 * side)
    left = left_blocks.reshape(2, LEFT_ROWS, side).transpose(1, 0, 2).reshape(LEFT_ROWS, 2 * side)
    left_all, right_all = exchange(rows, cols, left, right)
    total = product_sums(
        left_slots.reshape(PANELS, PRODUCTS), right_slots.reshape(PANELS, PRODUCTS),
        sink_slots.reshape(PANELS, PRODUCTS), live_counts.reshape(PANELS), left_all, right_all)
    return total.reshape(1, 1, SINK_SLOTS, side * side)


def solution(mesh):
    return jax.shard_map(
        functools.partial(per_device, mesh.shape["row"], mesh.shape["col"]),
        mesh=mesh,
        in_specs=(
            P("row", "col", None, None),
            P("row", "col", None, None),
            P("row", "col", None, None, None),
            P("row", "col", None, None, None),
            P("row", "col", None, None, None),
            P("row", "col", None, None),
        ),
        out_specs=P("row", "col", None, None),
        check_vma=False,
    )
```

```python
import functools

import jax
import jax.numpy as jnp
from jax import lax
from jax.experimental import pallas as pl
from jax.experimental.pallas import tpu as pltpu
from jax.sharding import PartitionSpec as P

TILE_SIDE = 64
LEFT_SLOTS = 4
RIGHT_SLOTS = 20
SINK_SLOTS = 12
PRODUCTS = 24
SECTIONS = 4
PANELS = 2 * SECTIONS
CHUNKS = 4
LEFT_ROWS = LEFT_SLOTS * TILE_SIDE
RIGHT_ROWS = RIGHT_SLOTS * TILE_SIDE // 2
CHUNK_ROWS = RIGHT_ROWS // CHUNKS
TURNED = CHUNKS // 2
MESH = pl.DeviceIdType.MESH


def chosen(column, values):
    total = 0
    for place, value in enumerate(values):
        if value:
            total = total + (column % len(values) == place).astype(jnp.int32) * value
    return total


def exchange_kernel(rows, cols, left_ref, right_ref, left_all, right_all, relay,
                    left_send, left_recv, entry_send, right_recv, down_send, up_send,
                    relay_send, relay_recv):
    row = lax.axis_index("row")
    column = lax.axis_index("col")
    parity = row % 2
    half_row = row // 2
    below = (row + rows - 1) % rows
    above = (row + 1) % rows
    offset = chosen(column, (0, 0, 0, 6, 6, 6, 4, 2))
    turned_offset = chosen(column, (0, 6, 0, 6, 0, 6, 4, 2))
    relay_shift = chosen(column, (0, rows - 4, 0, 0, 4, 0, 0, 0))
    relays = relay_shift != 0
    shift = (2 * column + offset) % rows
    final_shift = (2 * column + turned_offset + rows - relay_shift) % rows
    moves = shift != 0
    greets_final = relays & (final_shift != relay_shift)

    def greet(row_to, column_to):
        pl.semaphore_signal(barrier, inc=1, device_id=(row_to, column_to), device_id_type=MESH)

    barrier = pltpu.get_barrier_semaphore()
    greet(below, column)
    greet(above, column)

    @pl.when(moves)
    def _():
        greet((row + shift) % rows, column)

    @pl.when(relays)
    def _():
        greet((row + relay_shift) % rows, column)

    @pl.when(greets_final)
    def _():
        greet((row + final_shift) % rows, column)

    for section in range(SECTIONS):
        @pl.when((half_row + section) % cols != 0)
        def _():
            greet(row, (column + half_row + section) % cols)

    peers = 2 + moves.astype(jnp.int32) + relays.astype(jnp.int32) + greets_final.astype(jnp.int32)
    for section in range(SECTIONS):
        peers += ((half_row + section) % cols != 0).astype(jnp.int32)
    pl.semaphore_wait(barrier, peers)

    def entry_of(chunk):
        if isinstance(chunk, int):
            return parity + (turned_offset if chunk < TURNED else offset)
        return parity + offset + (chunk < TURNED).astype(jnp.int32) * (turned_offset - offset)

    def part(chunk):
        return pl.ds(pl.multiple_of(chunk * CHUNK_ROWS, 8), CHUNK_ROWS)

    def entry_copy(chunk):
        return pltpu.make_async_remote_copy(
            src_ref=right_ref.at[part(chunk)], dst_ref=right_all.at[entry_of(chunk), part(chunk)],
            send_sem=entry_send.at[chunk], recv_sem=right_recv.at[entry_of(chunk), chunk],
            device_id=((row + rows - shift) % rows, column), device_id_type=MESH)

    def local_copy(chunk):
        return pltpu.make_async_copy(
            right_ref.at[part(chunk)], right_all.at[entry_of(chunk), part(chunk)],
            right_recv.at[entry_of(chunk), chunk])

    def relay_copy(chunk):
        return pltpu.make_async_remote_copy(
            src_ref=right_ref.at[part(chunk)], dst_ref=relay.at[part(chunk)],
            send_sem=entry_send.at[chunk], recv_sem=relay_recv.at[chunk],
            device_id=((row + rows - relay_shift) % rows, column), device_id_type=MESH)

    def final_copy(chunk):
        return pltpu.make_async_remote_copy(
            src_ref=relay.at[part(chunk)], dst_ref=right_all.at[entry_of(chunk), part(chunk)],
            send_sem=relay_send.at[chunk], recv_sem=right_recv.at[entry_of(chunk), chunk],
            device_id=((row + rows - final_shift) % rows, column), device_id_type=MESH)

    def left_copy(section):
        target = (column + 2 * cols - half_row - section) % cols
        return pltpu.make_async_remote_copy(
            src_ref=left_ref, dst_ref=left_all.at[section],
            send_sem=left_send.at[section], recv_sem=left_recv.at[section],
            device_id=(row, target), device_id_type=MESH)

    def left_local(section):
        return pltpu.make_async_copy(left_ref, left_all.at[section], left_recv.at[section])

    def down_copy(slot, chunk):
        return pltpu.make_async_remote_copy(
            src_ref=right_all.at[slot, part(chunk)],
            dst_ref=right_all.at[slot + 2 * (1 - parity), part(chunk)],
            send_sem=down_send.at[slot, chunk],
            recv_sem=right_recv.at[slot + 2 * (1 - parity), chunk],
            device_id=(below, column), device_id_type=MESH)

    def up_copy(slot, chunk):
        return pltpu.make_async_remote_copy(
            src_ref=right_all.at[slot, part(chunk)],
            dst_ref=right_all.at[slot - 2 * parity, part(chunk)],
            send_sem=up_send.at[slot, chunk],
            recv_sem=right_recv.at[slot - 2 * parity, chunk],
            device_id=(above, column), device_id_type=MESH)

    for chunk in range(CHUNKS):
        direct = moves if chunk >= TURNED else moves & jnp.logical_not(relays)

        @pl.when(direct)
        def _():
            entry_copy(chunk).start()

        @pl.when(jnp.logical_not(moves))
        def _():
            local_copy(chunk).start()

        if chunk < TURNED:
            @pl.when(relays)
            def _():
                relay_copy(chunk).start()

    for section in range(SECTIONS):
        @pl.when((half_row + section) % cols != 0)
        def _():
            left_copy(section).start()

        @pl.when((half_row + section) % cols == 0)
        def _():
            left_local(section).start()

    last_down = PANELS - 1 - 2 * (1 - parity)
    last_up = 2 * parity

    def arrived(slot, chunk):
        pltpu.make_async_copy(
            right_ref.at[part(chunk)], right_all.at[slot, part(chunk)], right_recv.at[slot, chunk]).wait()

    def first(chunk, carry):
        entry = entry_of(chunk)
        arrived(entry, chunk)

        @pl.when(entry <= last_down)
        def _():
            down_copy(entry, chunk).start()

        @pl.when(entry >= last_up)
        def _():
            up_copy(entry, chunk).start()
        return carry

    lax.fori_loop(TURNED, CHUNKS, first, 0)

    @pl.when(relays)
    def _():
        for chunk in range(TURNED):
            relay_copy(chunk).wait_recv()
            final_copy(chunk).start()

    lax.fori_loop(0, TURNED, first, 0)

    def onward(step, carry):
        distance = step // CHUNKS + 1
        chunk = (step + TURNED) % CHUNKS
        higher = entry_of(chunk) + distance
        lower = entry_of(chunk) - distance

        @pl.when(higher < PANELS)
        def _():
            arrived(higher, chunk)

        @pl.when(higher <= last_down)
        def _():
            down_copy(higher, chunk).start()

        @pl.when(lower >= 0)
        def _():
            arrived(lower, chunk)

        @pl.when(lower >= last_up)
        def _():
            up_copy(lower, chunk).start()
        return carry

    lax.fori_loop(0, (PANELS - 1) * CHUNKS, onward, 0)

    def sent(step, carry):
        slot = step // CHUNKS
        chunk = step % CHUNKS
        entry = entry_of(chunk)

        @pl.when((slot >= entry) & (slot <= last_down))
        def _():
            down_copy(slot, chunk).wait_send()

        @pl.when((slot <= entry) & (slot >= last_up))
        def _():
            up_copy(slot, chunk).wait_send()
        return carry

    lax.fori_loop(0, PANELS * CHUNKS, sent, 0)

    for chunk in range(CHUNKS):
        @pl.when(moves)
        def _():
            entry_copy(chunk).wait_send()

        if chunk < TURNED:
            @pl.when(relays)
            def _():
                final_copy(chunk).wait_send()

    for section in range(SECTIONS):
        @pl.when((half_row + section) % cols != 0)
        def _():
            left_copy(section).wait()

        @pl.when((half_row + section) % cols == 0)
        def _():
            left_local(section).wait()


def exchange(rows, cols, left, right):
    dma = pltpu.SemaphoreType.DMA
    return pl.pallas_call(
        functools.partial(exchange_kernel, rows, cols),
        out_shape=(
            jax.ShapeDtypeStruct((SECTIONS, LEFT_ROWS, 2 * TILE_SIDE), jnp.float32),
            jax.ShapeDtypeStruct((PANELS, RIGHT_ROWS, 2 * TILE_SIDE), jnp.float32),
        ),
        in_specs=[pl.BlockSpec(memory_space=pltpu.VMEM)] * 2,
        out_specs=(pl.BlockSpec(memory_space=pltpu.VMEM),) * 2,
        scratch_shapes=[
            pltpu.VMEM((TURNED * CHUNK_ROWS, 2 * TILE_SIDE), jnp.float32),
            dma((SECTIONS,)), dma((SECTIONS,)), dma((CHUNKS,)), dma((PANELS, CHUNKS)),
            dma((PANELS, CHUNKS)), dma((PANELS, CHUNKS)), dma((TURNED,)), dma((TURNED,)),
        ],
        compiler_params=pltpu.CompilerParams(collective_id=0, has_side_effects=True),
        name="exchange",
    )(left, right)


def product_kernel(left_lists, right_lists, sink_lists, counts, left_all, right_all, out, products, sums):
    side = TILE_SIDE
    section = pl.program_id(0)

    @pl.when(section == 0)
    def _():
        sums[...] = jnp.zeros_like(sums)

    def ordered(count):
        return lax.broadcasted_iota(jnp.int32, (count, 2 * side), 1) < side

    place = lax.broadcasted_iota(jnp.int32, (2 * side, 2 * side), 0)
    target = lax.broadcasted_iota(jnp.int32, (2 * side, 2 * side), 1)
    moved = (place & side) + (place & 1) * (side // 2) + ((place & (side - 1)) >> 1)
    evens_first = (moved == target).astype(jnp.float32).astype(jnp.bfloat16)
    rows = LEFT_ROWS // 2
    low_lanes, low_lanes_left = ordered(side // 2), ordered(rows)
    for half in range(2):
        left = left_all[0, pl.ds(half * rows, rows), :]
        turned = pltpu.roll(left, side, 1)
        even = jnp.where(low_lanes_left, left, turned).reshape(LEFT_SLOTS, side // 2, 2 * side)
        odd = jnp.where(low_lanes_left, turned, left).reshape(LEFT_SLOTS, side // 2, 2 * side)
        twice = jnp.concatenate([even, odd], axis=1).reshape(LEFT_ROWS, 2 * side)
        high = twice.astype(jnp.bfloat16).astype(jnp.float32)
        split = jnp.where(ordered(LEFT_ROWS), high, twice - high).astype(jnp.bfloat16)
        split = jnp.dot(split, evens_first, preferred_element_type=jnp.float32).astype(jnp.bfloat16)
        stream = jnp.concatenate([split, split], axis=1)
        item = 2 * section + half
        for quad in range(RIGHT_SLOTS // 4):
            pairs = []
            for pair in range(2):
                base = (4 * quad + 2 * pair) * (side // 2)
                first = right_all[half, pl.ds(base, side // 2), :]
                second = right_all[half, pl.ds(base + side // 2, side // 2), :]
                pairs.append(jnp.concatenate([
                    jnp.where(low_lanes, first, pltpu.roll(second, side, 1)),
                    jnp.where(low_lanes, pltpu.roll(first, side, 1), second)], axis=0))
            right = jnp.concatenate(pairs, axis=1)
            right_high = right.astype(jnp.bfloat16)
            right_low = (right - right_high.astype(jnp.float32)).astype(jnp.bfloat16)
            held = jnp.concatenate([right_high, right_high, right_low, right_low], axis=0)
            found = jnp.dot(stream, held, preferred_element_type=jnp.float32)
            for n in range(2):
                products[pl.ds(LEFT_SLOTS * (2 * quad + n), LEFT_SLOTS)] = (
                    found[:, 2 * side * n : 2 * side * (n + 1)].reshape(LEFT_SLOTS, side, 2 * side))

        def add(position, inner):
            right_slot = right_lists[item, position]
            source = LEFT_SLOTS * (right_slot >> 1) + left_lists[item, position]
            sink = 2 * sink_lists[item, position] + (right_slot & 1)
            sums[sink] += products[source]
            return inner

        lax.fori_loop(0, counts[item], add, 0)

    @pl.when(section == SECTIONS - 1)
    def _():
        for sink in range(SINK_SLOTS):
            total = sums[2 * sink] + pltpu.roll(sums[2 * sink + 1], side, 1)
            out[pl.ds(sink * (side // 2), side // 2), :] = jnp.where(
                low_lanes, total[: side // 2], pltpu.roll(total[side // 2 :], side, 1))


def product_sums(left_lists, right_lists, sink_lists, counts, left_all, right_all):
    smem = pl.BlockSpec(memory_space=pltpu.SMEM)
    return pl.pallas_call(
        product_kernel,
        out_shape=jax.ShapeDtypeStruct((SINK_SLOTS * TILE_SIDE // 2, 2 * TILE_SIDE), jnp.float32),
        grid=(SECTIONS,),
        in_specs=[smem] * 4 + [
            pl.BlockSpec((1, LEFT_ROWS, 2 * TILE_SIDE), lambda section: (section, 0, 0)),
            pl.BlockSpec((2, RIGHT_ROWS, 2 * TILE_SIDE), lambda section: (section, 0, 0)),
        ],
        out_specs=pl.BlockSpec((SINK_SLOTS * TILE_SIDE // 2, 2 * TILE_SIDE), lambda section: (0, 0)),
        scratch_shapes=[
            pltpu.VMEM((LEFT_SLOTS * RIGHT_SLOTS // 2, TILE_SIDE, 2 * TILE_SIDE), jnp.float32),
            pltpu.VMEM((2 * SINK_SLOTS, TILE_SIDE, 2 * TILE_SIDE), jnp.float32),
        ],
        name="product_sums",
    )(left_lists, right_lists, sink_lists, counts, left_all, right_all)


def per_device(rows, cols, left_blocks, right_blocks, left_slots, right_slots, sink_slots, live_counts):
    right = right_blocks.reshape(RIGHT_ROWS, 2 * TILE_SIDE)
    left = left_blocks.reshape(LEFT_ROWS, 2 * TILE_SIDE)
    left_all, right_all = exchange(rows, cols, left, right)
    total = product_sums(
        left_slots.reshape(PANELS, PRODUCTS), right_slots.reshape(PANELS, PRODUCTS),
        sink_slots.reshape(PANELS, PRODUCTS), live_counts.reshape(PANELS), left_all, right_all)
    return total.reshape(1, 1, SINK_SLOTS, TILE_SIDE * TILE_SIDE)


def solution(mesh):
    return jax.shard_map(
        functools.partial(per_device, mesh.shape["row"], mesh.shape["col"]),
        mesh=mesh,
        in_specs=(
            P("row", "col", None, None),
            P("row", "col", None, None),
            P("row", "col", None, None, None),
            P("row", "col", None, None, None),
            P("row", "col", None, None, None),
            P("row", "col", None, None),
        ),
        out_specs=P("row", "col", None, None),
        check_vma=False,
    )
```

```python
import functools

import jax
import jax.numpy as jnp
from jax import lax
from jax.experimental import pallas as pl
from jax.experimental.pallas import tpu as pltpu
from jax.sharding import PartitionSpec as P

TILE_SIDE = 64
LEFT_SLOTS = 4
RIGHT_SLOTS = 20
SINK_SLOTS = 12
PRODUCTS = 24
SECTIONS = 4
PANELS = 2 * SECTIONS
CHUNKS = 4
LEFT_ROWS = LEFT_SLOTS * TILE_SIDE
RIGHT_ROWS = RIGHT_SLOTS * TILE_SIDE // 2
CHUNK_ROWS = RIGHT_ROWS // CHUNKS
TURNED = CHUNKS // 2
DETOURS = PANELS - 2
OFFSETS = (0, 0, 0, 6, 6, 6, 4, 2)
TURNED_OFFSETS = (0, 6, 0, 6, 0, 6, 4, 2)
MESH = pl.DeviceIdType.MESH


def chosen(column, values):
    total = 0
    for place, value in enumerate(values):
        if value:
            total = total + (column % len(values) == place).astype(jnp.int32) * value
    return total


def exchange_kernel(rows, cols, left_ref, right_ref, left_all, right_all, relay,
                    left_send, left_recv, entry_send, right_recv, down_send, up_send,
                    relay_send, relay_recv, detour, detour_send, detour_recv):
    row = lax.axis_index("row")
    column = lax.axis_index("col")
    parity = row % 2
    half_row = row // 2
    below = (row + rows - 1) % rows
    above = (row + 1) % rows
    offset = chosen(column, OFFSETS)
    turned_offset = chosen(column, TURNED_OFFSETS)
    relay_shift = chosen(column, (0, rows - 4, 0, 0, 4, 0, 0, 0))
    relays = relay_shift != 0
    shift = (2 * column + offset) % rows
    final_shift = (2 * column + turned_offset + rows - relay_shift) % rows
    moves = shift != 0
    greets_final = relays & (final_shift != relay_shift)

    half = rows // 2
    at_low = row % half == 0
    at_high = row % half == half - 1
    at_edge = at_low | at_high
    y_low = column // 2 % 2
    back_row = (row + half * (1 - y_low)) % rows
    back_column = (column + 2 - 4 * y_low) % cols
    ahead_row = (row + half * y_low) % rows
    ahead_column = back_column
    onto_row = (ahead_row + rows + 1 - 2 * at_low.astype(jnp.int32)) % rows
    opposite_row = (ahead_row + (half - 1) * (at_low.astype(jnp.int32) - at_high.astype(jnp.int32)) + rows) % rows

    def greet(row_to, column_to):
        pl.semaphore_signal(barrier, inc=1, device_id=(row_to, column_to), device_id_type=MESH)

    barrier = pltpu.get_barrier_semaphore()
    greet(below, column)
    greet(above, column)

    @pl.when(moves)
    def _():
        greet((row + shift) % rows, column)

    @pl.when(relays)
    def _():
        greet((row + relay_shift) % rows, column)

    @pl.when(greets_final)
    def _():
        greet((row + final_shift) % rows, column)

    @pl.when(at_edge)
    def _():
        greet(ahead_row, ahead_column)
        greet(opposite_row, ahead_column)

    for section in range(SECTIONS):
        @pl.when((half_row + section) % cols != 0)
        def _():
            greet(row, (column + half_row + section) % cols)

    peers = 2 + moves.astype(jnp.int32) + relays.astype(jnp.int32) + greets_final.astype(jnp.int32)
    peers += 2 * at_edge.astype(jnp.int32)
    for section in range(SECTIONS):
        peers += ((half_row + section) % cols != 0).astype(jnp.int32)
    pl.semaphore_wait(barrier, peers)

    def entry_of(chunk):
        if isinstance(chunk, int):
            return parity + (turned_offset if chunk < TURNED else offset)
        return parity + offset + (chunk < TURNED).astype(jnp.int32) * (turned_offset - offset)

    def part(chunk):
        return pl.ds(pl.multiple_of(chunk * CHUNK_ROWS, 8), CHUNK_ROWS)

    def entry_copy(chunk):
        return pltpu.make_async_remote_copy(
            src_ref=right_ref.at[part(chunk)], dst_ref=right_all.at[entry_of(chunk), part(chunk)],
            send_sem=entry_send.at[chunk], recv_sem=right_recv.at[entry_of(chunk), chunk],
            device_id=((row + rows - shift) % rows, column), device_id_type=MESH)

    def local_copy(chunk):
        return pltpu.make_async_copy(
            right_ref.at[part(chunk)], right_all.at[entry_of(chunk), part(chunk)],
            right_recv.at[entry_of(chunk), chunk])

    def relay_copy(chunk):
        return pltpu.make_async_remote_copy(
            src_ref=right_ref.at[part(chunk)], dst_ref=relay.at[part(chunk)],
            send_sem=entry_send.at[chunk], recv_sem=relay_recv.at[chunk],
            device_id=((row + rows - relay_shift) % rows, column), device_id_type=MESH)

    def final_copy(chunk):
        return pltpu.make_async_remote_copy(
            src_ref=relay.at[part(chunk)], dst_ref=right_all.at[entry_of(chunk), part(chunk)],
            send_sem=relay_send.at[chunk], recv_sem=right_recv.at[entry_of(chunk), chunk],
            device_id=((row + rows - final_shift) % rows, column), device_id_type=MESH)

    def left_copy(section):
        target = (column + 2 * cols - half_row - section) % cols
        return pltpu.make_async_remote_copy(
            src_ref=left_ref, dst_ref=left_all.at[section],
            send_sem=left_send.at[section], recv_sem=left_recv.at[section],
            device_id=(row, target), device_id_type=MESH)

    def left_local(section):
        return pltpu.make_async_copy(left_ref, left_all.at[section], left_recv.at[section])

    def down_copy(slot, chunk):
        return pltpu.make_async_remote_copy(
            src_ref=right_all.at[slot, part(chunk)],
            dst_ref=right_all.at[slot + 2 * (1 - parity), part(chunk)],
            send_sem=down_send.at[slot, chunk],
            recv_sem=right_recv.at[slot + 2 * (1 - parity), chunk],
            device_id=(below, column), device_id_type=MESH)

    def up_copy(slot, chunk):
        return pltpu.make_async_remote_copy(
            src_ref=right_all.at[slot, part(chunk)],
            dst_ref=right_all.at[slot - 2 * parity, part(chunk)],
            send_sem=up_send.at[slot, chunk],
            recv_sem=right_recv.at[slot - 2 * parity, chunk],
            device_id=(above, column), device_id_type=MESH)

    def start_down(slot, chunk):
        odd = at_low & (chunk % 2 == 1)

        @pl.when(odd)
        def _():
            detour_copy(slot, chunk, slot - entry_of(chunk), down_send).start()

        @pl.when(jnp.logical_not(odd))
        def _():
            down_copy(slot, chunk).start()

    def start_up(slot, chunk):
        odd = at_high & (chunk % 2 == 1)

        @pl.when(odd)
        def _():
            detour_copy(slot, chunk, entry_of(chunk) - slot, up_send).start()

        @pl.when(jnp.logical_not(odd))
        def _():
            up_copy(slot, chunk).start()

    def detour_copy(slot, chunk, place, send_sem):
        return pltpu.make_async_remote_copy(
            src_ref=right_all.at[slot, part(chunk)], dst_ref=detour.at[place, chunk // 2],
            send_sem=send_sem.at[slot, chunk], recv_sem=detour_recv.at[place, chunk // 2],
            device_id=(back_row, back_column), device_id_type=MESH)

    ahead_offset = chosen(ahead_column, OFFSETS)
    ahead_turned = chosen(ahead_column, TURNED_OFFSETS)
    low = at_low.astype(jnp.int32)

    def ahead_slot(chunk, place):
        entry = parity + ahead_offset + (chunk < TURNED).astype(jnp.int32) * (ahead_turned - ahead_offset)
        return entry + place * (2 * low - 1)

    def passes(chunk, place):
        slot = ahead_slot(chunk, place)
        return at_edge & (chunk % 2 == 1) & (at_low & (slot <= PANELS - 3) | at_high & (slot >= 2))

    def passed_copy(chunk, place):
        slot = ahead_slot(chunk, place) + 2 * (2 * low - 1)
        return pltpu.make_async_remote_copy(
            src_ref=detour.at[place, chunk // 2], dst_ref=right_all.at[slot, part(chunk)],
            send_sem=detour_send.at[place, chunk // 2], recv_sem=right_recv.at[slot, chunk],
            device_id=(onto_row, ahead_column), device_id_type=MESH)

    for chunk in range(CHUNKS):
        direct = moves if chunk >= TURNED else moves & jnp.logical_not(relays)

        @pl.when(direct)
        def _():
            entry_copy(chunk).start()

        @pl.when(jnp.logical_not(moves))
        def _():
            local_copy(chunk).start()

        if chunk < TURNED:
            @pl.when(relays)
            def _():
                relay_copy(chunk).start()

    for section in range(SECTIONS):
        @pl.when((half_row + section) % cols != 0)
        def _():
            left_copy(section).start()

        @pl.when((half_row + section) % cols == 0)
        def _():
            left_local(section).start()

    last_down = PANELS - 1 - 2 * (1 - parity)
    last_up = 2 * parity

    def arrived(slot, chunk):
        pltpu.make_async_copy(
            right_ref.at[part(chunk)], right_all.at[slot, part(chunk)], right_recv.at[slot, chunk]).wait()

    def first(chunk, carry):
        entry = entry_of(chunk)
        arrived(entry, chunk)

        @pl.when(entry <= last_down)
        def _():
            start_down(entry, chunk)

        @pl.when(entry >= last_up)
        def _():
            start_up(entry, chunk)
        return carry

    lax.fori_loop(TURNED, CHUNKS, first, 0)

    @pl.when(relays)
    def _():
        for chunk in range(TURNED):
            relay_copy(chunk).wait_recv()
            final_copy(chunk).start()

    lax.fori_loop(0, TURNED, first, 0)

    def onward(step, carry):
        distance = step // CHUNKS + 1
        chunk = (step + TURNED) % CHUNKS
        higher = entry_of(chunk) + distance
        lower = entry_of(chunk) - distance

        @pl.when(passes(chunk, distance - 1) & (distance <= DETOURS))
        def _():
            pltpu.make_async_copy(
                right_ref.at[part(chunk)], detour.at[distance - 1, chunk // 2],
                detour_recv.at[distance - 1, chunk // 2]).wait()
            passed_copy(chunk, distance - 1).start()

        @pl.when(higher < PANELS)
        def _():
            arrived(higher, chunk)

        @pl.when(higher <= last_down)
        def _():
            start_down(higher, chunk)

        @pl.when(lower >= 0)
        def _():
            arrived(lower, chunk)

        @pl.when(lower >= last_up)
        def _():
            start_up(lower, chunk)
        return carry

    lax.fori_loop(0, (PANELS - 1) * CHUNKS, onward, 0)

    def passed(step, carry):
        chunk = step % CHUNKS
        place = step // CHUNKS

        @pl.when(passes(chunk, place))
        def _():
            passed_copy(chunk, place).wait_send()
        return carry

    lax.fori_loop(0, DETOURS * CHUNKS, passed, 0)

    def sent(step, carry):
        slot = step // CHUNKS
        chunk = step % CHUNKS
        entry = entry_of(chunk)

        @pl.when((slot >= entry) & (slot <= last_down))
        def _():
            down_copy(slot, chunk).wait_send()

        @pl.when((slot <= entry) & (slot >= last_up))
        def _():
            up_copy(slot, chunk).wait_send()
        return carry

    lax.fori_loop(0, PANELS * CHUNKS, sent, 0)

    for chunk in range(CHUNKS):
        @pl.when(moves)
        def _():
            entry_copy(chunk).wait_send()

        if chunk < TURNED:
            @pl.when(relays)
            def _():
                final_copy(chunk).wait_send()

    for section in range(SECTIONS):
        @pl.when((half_row + section) % cols != 0)
        def _():
            left_copy(section).wait()

        @pl.when((half_row + section) % cols == 0)
        def _():
            left_local(section).wait()


def exchange(rows, cols, left, right):
    dma = pltpu.SemaphoreType.DMA
    return pl.pallas_call(
        functools.partial(exchange_kernel, rows, cols),
        out_shape=(
            jax.ShapeDtypeStruct((SECTIONS, LEFT_ROWS, 2 * TILE_SIDE), jnp.float32),
            jax.ShapeDtypeStruct((PANELS, RIGHT_ROWS, 2 * TILE_SIDE), jnp.float32),
        ),
        in_specs=[pl.BlockSpec(memory_space=pltpu.VMEM)] * 2,
        out_specs=(pl.BlockSpec(memory_space=pltpu.VMEM),) * 2,
        scratch_shapes=[
            pltpu.VMEM((TURNED * CHUNK_ROWS, 2 * TILE_SIDE), jnp.float32),
            dma((SECTIONS,)), dma((SECTIONS,)), dma((CHUNKS,)), dma((PANELS, CHUNKS)),
            dma((PANELS, CHUNKS)), dma((PANELS, CHUNKS)), dma((TURNED,)), dma((TURNED,)),
            pltpu.VMEM((DETOURS, CHUNKS // 2, CHUNK_ROWS, 2 * TILE_SIDE), jnp.float32),
            dma((DETOURS, CHUNKS // 2)), dma((DETOURS, CHUNKS // 2)),
        ],
        compiler_params=pltpu.CompilerParams(collective_id=0, has_side_effects=True),
        name="exchange",
    )(left, right)


def product_kernel(left_lists, right_lists, sink_lists, counts, left_all, right_all, out, products, sums):
    side = TILE_SIDE
    section = pl.program_id(0)

    @pl.when(section == 0)
    def _():
        sums[...] = jnp.zeros_like(sums)

    def ordered(count):
        return lax.broadcasted_iota(jnp.int32, (count, 2 * side), 1) < side

    place = lax.broadcasted_iota(jnp.int32, (2 * side, 2 * side), 0)
    target = lax.broadcasted_iota(jnp.int32, (2 * side, 2 * side), 1)
    moved = (place & side) + (place & 1) * (side // 2) + ((place & (side - 1)) >> 1)
    evens_first = (moved == target).astype(jnp.float32).astype(jnp.bfloat16)
    rows = LEFT_ROWS // 2
    low_lanes, low_lanes_left = ordered(side // 2), ordered(rows)
    for half in range(2):
        left = left_all[0, pl.ds(half * rows, rows), :]
        turned = pltpu.roll(left, side, 1)
        even = jnp.where(low_lanes_left, left, turned).reshape(LEFT_SLOTS, side // 2, 2 * side)
        odd = jnp.where(low_lanes_left, turned, left).reshape(LEFT_SLOTS, side // 2, 2 * side)
        twice = jnp.concatenate([even, odd], axis=1).reshape(LEFT_ROWS, 2 * side)
        high = twice.astype(jnp.bfloat16).astype(jnp.float32)
        split = jnp.where(ordered(LEFT_ROWS), high, twice - high).astype(jnp.bfloat16)
        split = jnp.dot(split, evens_first, preferred_element_type=jnp.float32).astype(jnp.bfloat16)
        stream = jnp.concatenate([split, split], axis=1)
        item = 2 * section + half
        for quad in range(RIGHT_SLOTS // 4):
            pairs = []
            for pair in range(2):
                base = (4 * quad + 2 * pair) * (side // 2)
                first = right_all[half, pl.ds(base, side // 2), :]
                second = right_all[half, pl.ds(base + side // 2, side // 2), :]
                pairs.append(jnp.concatenate([
                    jnp.where(low_lanes, first, pltpu.roll(second, side, 1)),
                    jnp.where(low_lanes, pltpu.roll(first, side, 1), second)], axis=0))
            right = jnp.concatenate(pairs, axis=1)
            right_high = right.astype(jnp.bfloat16)
            right_low = (right - right_high.astype(jnp.float32)).astype(jnp.bfloat16)
            held = jnp.concatenate([right_high, right_high, right_low, right_low], axis=0)
            found = jnp.dot(stream, held, preferred_element_type=jnp.float32)
            for n in range(2):
                products[pl.ds(LEFT_SLOTS * (2 * quad + n), LEFT_SLOTS)] = (
                    found[:, 2 * side * n : 2 * side * (n + 1)].reshape(LEFT_SLOTS, side, 2 * side))

        def add(position, inner):
            right_slot = right_lists[item, position]
            source = LEFT_SLOTS * (right_slot >> 1) + left_lists[item, position]
            sink = 2 * sink_lists[item, position] + (right_slot & 1)
            sums[sink] += products[source]
            return inner

        lax.fori_loop(0, counts[item], add, 0)

    @pl.when(section == SECTIONS - 1)
    def _():
        for sink in range(SINK_SLOTS):
            total = sums[2 * sink] + pltpu.roll(sums[2 * sink + 1], side, 1)
            out[pl.ds(sink * (side // 2), side // 2), :] = jnp.where(
                low_lanes, total[: side // 2], pltpu.roll(total[side // 2 :], side, 1))


def product_sums(left_lists, right_lists, sink_lists, counts, left_all, right_all):
    smem = pl.BlockSpec(memory_space=pltpu.SMEM)
    return pl.pallas_call(
        product_kernel,
        out_shape=jax.ShapeDtypeStruct((SINK_SLOTS * TILE_SIDE // 2, 2 * TILE_SIDE), jnp.float32),
        grid=(SECTIONS,),
        in_specs=[smem] * 4 + [
            pl.BlockSpec((1, LEFT_ROWS, 2 * TILE_SIDE), lambda section: (section, 0, 0)),
            pl.BlockSpec((2, RIGHT_ROWS, 2 * TILE_SIDE), lambda section: (section, 0, 0)),
        ],
        out_specs=pl.BlockSpec((SINK_SLOTS * TILE_SIDE // 2, 2 * TILE_SIDE), lambda section: (0, 0)),
        scratch_shapes=[
            pltpu.VMEM((LEFT_SLOTS * RIGHT_SLOTS // 2, TILE_SIDE, 2 * TILE_SIDE), jnp.float32),
            pltpu.VMEM((2 * SINK_SLOTS, TILE_SIDE, 2 * TILE_SIDE), jnp.float32),
        ],
        name="product_sums",
    )(left_lists, right_lists, sink_lists, counts, left_all, right_all)


def per_device(rows, cols, left_blocks, right_blocks, left_slots, right_slots, sink_slots, live_counts):
    right = right_blocks.reshape(RIGHT_ROWS, 2 * TILE_SIDE)
    left = left_blocks.reshape(LEFT_ROWS, 2 * TILE_SIDE)
    left_all, right_all = exchange(rows, cols, left, right)
    total = product_sums(
        left_slots.reshape(PANELS, PRODUCTS), right_slots.reshape(PANELS, PRODUCTS),
        sink_slots.reshape(PANELS, PRODUCTS), live_counts.reshape(PANELS), left_all, right_all)
    return total.reshape(1, 1, SINK_SLOTS, TILE_SIDE * TILE_SIDE)


def solution(mesh):
    return jax.shard_map(
        functools.partial(per_device, mesh.shape["row"], mesh.shape["col"]),
        mesh=mesh,
        in_specs=(
            P("row", "col", None, None),
            P("row", "col", None, None),
            P("row", "col", None, None, None),
            P("row", "col", None, None, None),
            P("row", "col", None, None, None),
            P("row", "col", None, None),
        ),
        out_specs=P("row", "col", None, None),
        check_vma=False,
    )
```

```python
import functools

import jax
import jax.numpy as jnp
from jax import lax
from jax.experimental import pallas as pl
from jax.experimental.pallas import tpu as pltpu
from jax.sharding import PartitionSpec as P

TILE_SIDE = 64
LEFT_SLOTS = 4
RIGHT_SLOTS = 20
SINK_SLOTS = 12
PRODUCTS = 24
SECTIONS = 4
PANELS = 2 * SECTIONS
CHUNKS = 4
LEFT_ROWS = LEFT_SLOTS * TILE_SIDE
RIGHT_ROWS = RIGHT_SLOTS * TILE_SIDE // 2
CHUNK_ROWS = RIGHT_ROWS // CHUNKS
TURNED = CHUNKS // 2
MESH = pl.DeviceIdType.MESH


def chosen(column, values):
    total = 0
    for place, value in enumerate(values):
        if value:
            total = total + (column % len(values) == place).astype(jnp.int32) * value
    return total


def exchange_kernel(rows, cols, left_ref, right_ref, left_all, right_all, relay,
                    left_send, left_recv, entry_send, right_recv, down_send, up_send,
                    relay_send, relay_recv, early_send):
    row = lax.axis_index("row")
    column = lax.axis_index("col")
    parity = row % 2
    half_row = row // 2
    below = (row + rows - 1) % rows
    above = (row + 1) % rows
    offset = chosen(column, (0, 0, 0, 6, 6, 6, 4, 2))
    turned_offset = chosen(column, (0, 6, 0, 6, 0, 6, 4, 2))
    relay_shift = chosen(column, (0, rows - 4, 0, 0, 4, 0, 0, 0))
    relays = relay_shift != 0
    shift = (2 * column + offset) % rows
    final_shift = (2 * column + turned_offset + rows - relay_shift) % rows
    moves = shift != 0
    greets_final = relays & (final_shift != relay_shift)

    half = rows // 2
    at_low = row % half == 0
    at_high = row % half == half - 1
    before_low = row % half == 1
    before_high = row % half == half - 2

    def greet(row_to, column_to):
        pl.semaphore_signal(barrier, inc=1, device_id=(row_to, column_to), device_id_type=MESH)

    barrier = pltpu.get_barrier_semaphore()
    greet(below, column)
    greet(above, column)

    @pl.when(moves)
    def _():
        greet((row + shift) % rows, column)

    @pl.when(relays)
    def _():
        greet((row + relay_shift) % rows, column)

    @pl.when(greets_final)
    def _():
        greet((row + final_shift) % rows, column)

    @pl.when(at_high)
    def _():
        greet((row + 2) % rows, column)

    @pl.when(at_low)
    def _():
        greet((row + rows - 2) % rows, column)

    for section in range(SECTIONS):
        @pl.when((half_row + section) % cols != 0)
        def _():
            greet(row, (column + half_row + section) % cols)

    peers = 2 + moves.astype(jnp.int32) + relays.astype(jnp.int32) + greets_final.astype(jnp.int32)
    peers += before_low.astype(jnp.int32) + before_high.astype(jnp.int32)
    for section in range(SECTIONS):
        peers += ((half_row + section) % cols != 0).astype(jnp.int32)
    pl.semaphore_wait(barrier, peers)

    def entry_of(chunk):
        if isinstance(chunk, int):
            return parity + (turned_offset if chunk < TURNED else offset)
        return parity + offset + (chunk < TURNED).astype(jnp.int32) * (turned_offset - offset)

    def part(chunk):
        return pl.ds(pl.multiple_of(chunk * CHUNK_ROWS, 8), CHUNK_ROWS)

    def entry_copy(chunk):
        return pltpu.make_async_remote_copy(
            src_ref=right_ref.at[part(chunk)], dst_ref=right_all.at[entry_of(chunk), part(chunk)],
            send_sem=entry_send.at[chunk], recv_sem=right_recv.at[entry_of(chunk), chunk],
            device_id=((row + rows - shift) % rows, column), device_id_type=MESH)

    def local_copy(chunk):
        return pltpu.make_async_copy(
            right_ref.at[part(chunk)], right_all.at[entry_of(chunk), part(chunk)],
            right_recv.at[entry_of(chunk), chunk])

    def relay_copy(chunk):
        return pltpu.make_async_remote_copy(
            src_ref=right_ref.at[part(chunk)], dst_ref=relay.at[part(chunk)],
            send_sem=entry_send.at[chunk], recv_sem=relay_recv.at[chunk],
            device_id=((row + rows - relay_shift) % rows, column), device_id_type=MESH)

    def final_copy(chunk):
        return pltpu.make_async_remote_copy(
            src_ref=relay.at[part(chunk)], dst_ref=right_all.at[entry_of(chunk), part(chunk)],
            send_sem=relay_send.at[chunk], recv_sem=right_recv.at[entry_of(chunk), chunk],
            device_id=((row + rows - final_shift) % rows, column), device_id_type=MESH)

    def left_copy(section):
        target = (column + 2 * cols - half_row - section) % cols
        return pltpu.make_async_remote_copy(
            src_ref=left_ref, dst_ref=left_all.at[section],
            send_sem=left_send.at[section], recv_sem=left_recv.at[section],
            device_id=(row, target), device_id_type=MESH)

    def left_local(section):
        return pltpu.make_async_copy(left_ref, left_all.at[section], left_recv.at[section])

    def down_copy(slot, chunk):
        return pltpu.make_async_remote_copy(
            src_ref=right_all.at[slot, part(chunk)],
            dst_ref=right_all.at[slot + 2 * (1 - parity), part(chunk)],
            send_sem=down_send.at[slot, chunk],
            recv_sem=right_recv.at[slot + 2 * (1 - parity), chunk],
            device_id=(below, column), device_id_type=MESH)

    def up_copy(slot, chunk):
        return pltpu.make_async_remote_copy(
            src_ref=right_all.at[slot, part(chunk)],
            dst_ref=right_all.at[slot - 2 * parity, part(chunk)],
            send_sem=up_send.at[slot, chunk],
            recv_sem=right_recv.at[slot - 2 * parity, chunk],
            device_id=(above, column), device_id_type=MESH)

    def early_copy(slot):
        way = 1 - 2 * before_low.astype(jnp.int32)
        onto = slot - 2 * way
        return pltpu.make_async_remote_copy(
            src_ref=right_all.at[slot, part(CHUNKS - 1)], dst_ref=right_all.at[onto, part(CHUNKS - 1)],
            send_sem=early_send.at[slot], recv_sem=right_recv.at[onto, CHUNKS - 1],
            device_id=((row + rows + 2 * way) % rows, column), device_id_type=MESH)

    def sends_early(slot):
        entry = entry_of(CHUNKS - 1)
        return (before_low & (slot >= entry) & (slot <= PANELS - 3)) | (before_high & (slot <= entry) & (slot >= 2))

    def sends_down(slot, chunk):
        late = at_low & (chunk == CHUNKS - 1) & (slot != entry_of(chunk))
        return (slot <= last_down) & jnp.logical_not(late)

    def sends_up(slot, chunk):
        late = at_high & (chunk == CHUNKS - 1) & (slot != entry_of(chunk))
        return (slot >= last_up) & jnp.logical_not(late)

    last_down = PANELS - 1 - 2 * (1 - parity)
    last_up = 2 * parity

    for chunk in range(CHUNKS):
        direct = moves if chunk >= TURNED else moves & jnp.logical_not(relays)

        @pl.when(direct)
        def _():
            entry_copy(chunk).start()

        @pl.when(jnp.logical_not(moves))
        def _():
            local_copy(chunk).start()

        if chunk < TURNED:
            @pl.when(relays)
            def _():
                relay_copy(chunk).start()

    for section in range(SECTIONS):
        @pl.when((half_row + section) % cols != 0)
        def _():
            left_copy(section).start()

        @pl.when((half_row + section) % cols == 0)
        def _():
            left_local(section).start()

    def arrived(slot, chunk):
        pltpu.make_async_copy(
            right_ref.at[part(chunk)], right_all.at[slot, part(chunk)], right_recv.at[slot, chunk]).wait()

    def first(chunk, carry):
        entry = entry_of(chunk)
        arrived(entry, chunk)

        @pl.when((chunk == CHUNKS - 1) & sends_early(entry))
        def _():
            early_copy(entry).start()

        @pl.when(entry <= last_down)
        def _():
            down_copy(entry, chunk).start()

        @pl.when(entry >= last_up)
        def _():
            up_copy(entry, chunk).start()
        return carry

    lax.fori_loop(TURNED, CHUNKS, first, 0)

    @pl.when(relays)
    def _():
        for chunk in range(TURNED):
            relay_copy(chunk).wait_recv()
            final_copy(chunk).start()

    lax.fori_loop(0, TURNED, first, 0)

    def onward(step, carry):
        distance = step // CHUNKS + 1
        chunk = (step + TURNED) % CHUNKS
        higher = entry_of(chunk) + distance
        lower = entry_of(chunk) - distance

        @pl.when(higher < PANELS)
        def _():
            arrived(higher, chunk)

        @pl.when((chunk == CHUNKS - 1) & (higher < PANELS) & sends_early(higher))
        def _():
            early_copy(higher).start()

        @pl.when(sends_down(higher, chunk))
        def _():
            down_copy(higher, chunk).start()

        @pl.when(lower >= 0)
        def _():
            arrived(lower, chunk)

        @pl.when((chunk == CHUNKS - 1) & (lower >= 0) & sends_early(lower))
        def _():
            early_copy(lower).start()

        @pl.when(sends_up(lower, chunk))
        def _():
            up_copy(lower, chunk).start()
        return carry

    lax.fori_loop(0, (PANELS - 1) * CHUNKS, onward, 0)

    def sent(step, carry):
        slot = step // CHUNKS
        chunk = step % CHUNKS
        entry = entry_of(chunk)

        @pl.when((slot >= entry) & sends_down(slot, chunk))
        def _():
            down_copy(slot, chunk).wait_send()

        @pl.when((slot <= entry) & sends_up(slot, chunk))
        def _():
            up_copy(slot, chunk).wait_send()

        @pl.when((chunk == CHUNKS - 1) & sends_early(slot))
        def _():
            early_copy(slot).wait_send()
        return carry

    lax.fori_loop(0, PANELS * CHUNKS, sent, 0)

    for chunk in range(CHUNKS):
        @pl.when(moves)
        def _():
            entry_copy(chunk).wait_send()

        if chunk < TURNED:
            @pl.when(relays)
            def _():
                final_copy(chunk).wait_send()

    for section in range(SECTIONS):
        @pl.when((half_row + section) % cols != 0)
        def _():
            left_copy(section).wait()

        @pl.when((half_row + section) % cols == 0)
        def _():
            left_local(section).wait()


def exchange(rows, cols, left, right):
    dma = pltpu.SemaphoreType.DMA
    return pl.pallas_call(
        functools.partial(exchange_kernel, rows, cols),
        out_shape=(
            jax.ShapeDtypeStruct((SECTIONS, LEFT_ROWS, 2 * TILE_SIDE), jnp.float32),
            jax.ShapeDtypeStruct((PANELS, RIGHT_ROWS, 2 * TILE_SIDE), jnp.float32),
        ),
        in_specs=[pl.BlockSpec(memory_space=pltpu.VMEM)] * 2,
        out_specs=(pl.BlockSpec(memory_space=pltpu.VMEM),) * 2,
        scratch_shapes=[
            pltpu.VMEM((TURNED * CHUNK_ROWS, 2 * TILE_SIDE), jnp.float32),
            dma((SECTIONS,)), dma((SECTIONS,)), dma((CHUNKS,)), dma((PANELS, CHUNKS)),
            dma((PANELS, CHUNKS)), dma((PANELS, CHUNKS)), dma((TURNED,)), dma((TURNED,)), dma((PANELS,)),
        ],
        compiler_params=pltpu.CompilerParams(collective_id=0, has_side_effects=True),
        name="exchange",
    )(left, right)


def product_kernel(left_lists, right_lists, sink_lists, counts, left_all, right_all, out, products, sums):
    side = TILE_SIDE
    section = pl.program_id(0)

    @pl.when(section == 0)
    def _():
        sums[...] = jnp.zeros_like(sums)

    def ordered(count):
        return lax.broadcasted_iota(jnp.int32, (count, 2 * side), 1) < side

    place = lax.broadcasted_iota(jnp.int32, (2 * side, 2 * side), 0)
    target = lax.broadcasted_iota(jnp.int32, (2 * side, 2 * side), 1)
    moved = (place & side) + (place & 1) * (side // 2) + ((place & (side - 1)) >> 1)
    evens_first = (moved == target).astype(jnp.float32).astype(jnp.bfloat16)
    rows = LEFT_ROWS // 2
    low_lanes, low_lanes_left = ordered(side // 2), ordered(rows)
    for half in range(2):
        left = left_all[0, pl.ds(half * rows, rows), :]
        turned = pltpu.roll(left, side, 1)
        even = jnp.where(low_lanes_left, left, turned).reshape(LEFT_SLOTS, side // 2, 2 * side)
        odd = jnp.where(low_lanes_left, turned, left).reshape(LEFT_SLOTS, side // 2, 2 * side)
        twice = jnp.concatenate([even, odd], axis=1).reshape(LEFT_ROWS, 2 * side)
        high = twice.astype(jnp.bfloat16).astype(jnp.float32)
        split = jnp.where(ordered(LEFT_ROWS), high, twice - high).astype(jnp.bfloat16)
        split = jnp.dot(split, evens_first, preferred_element_type=jnp.float32).astype(jnp.bfloat16)
        stream = jnp.concatenate([split, split], axis=1)
        item = 2 * section + half
        for quad in range(RIGHT_SLOTS // 4):
            pairs = []
            for pair in range(2):
                base = (4 * quad + 2 * pair) * (side // 2)
                first = right_all[half, pl.ds(base, side // 2), :]
                second = right_all[half, pl.ds(base + side // 2, side // 2), :]
                pairs.append(jnp.concatenate([
                    jnp.where(low_lanes, first, pltpu.roll(second, side, 1)),
                    jnp.where(low_lanes, pltpu.roll(first, side, 1), second)], axis=0))
            right = jnp.concatenate(pairs, axis=1)
            right_high = right.astype(jnp.bfloat16)
            right_low = (right - right_high.astype(jnp.float32)).astype(jnp.bfloat16)
            held = jnp.concatenate([right_high, right_high, right_low, right_low], axis=0)
            found = jnp.dot(stream, held, preferred_element_type=jnp.float32)
            for n in range(2):
                products[pl.ds(LEFT_SLOTS * (2 * quad + n), LEFT_SLOTS)] = (
                    found[:, 2 * side * n : 2 * side * (n + 1)].reshape(LEFT_SLOTS, side, 2 * side))

        def add(position, inner):
            right_slot = right_lists[item, position]
            source = LEFT_SLOTS * (right_slot >> 1) + left_lists[item, position]
            sink = 2 * sink_lists[item, position] + (right_slot & 1)
            sums[sink] += products[source]
            return inner

        lax.fori_loop(0, counts[item], add, 0)

    @pl.when(section == SECTIONS - 1)
    def _():
        for sink in range(SINK_SLOTS):
            total = sums[2 * sink] + pltpu.roll(sums[2 * sink + 1], side, 1)
            out[pl.ds(sink * (side // 2), side // 2), :] = jnp.where(
                low_lanes, total[: side // 2], pltpu.roll(total[side // 2 :], side, 1))


def product_sums(left_lists, right_lists, sink_lists, counts, left_all, right_all):
    smem = pl.BlockSpec(memory_space=pltpu.SMEM)
    return pl.pallas_call(
        product_kernel,
        out_shape=jax.ShapeDtypeStruct((SINK_SLOTS * TILE_SIDE // 2, 2 * TILE_SIDE), jnp.float32),
        grid=(SECTIONS,),
        in_specs=[smem] * 4 + [
            pl.BlockSpec((1, LEFT_ROWS, 2 * TILE_SIDE), lambda section: (section, 0, 0)),
            pl.BlockSpec((2, RIGHT_ROWS, 2 * TILE_SIDE), lambda section: (section, 0, 0)),
        ],
        out_specs=pl.BlockSpec((SINK_SLOTS * TILE_SIDE // 2, 2 * TILE_SIDE), lambda section: (0, 0)),
        scratch_shapes=[
            pltpu.VMEM((LEFT_SLOTS * RIGHT_SLOTS // 2, TILE_SIDE, 2 * TILE_SIDE), jnp.float32),
            pltpu.VMEM((2 * SINK_SLOTS, TILE_SIDE, 2 * TILE_SIDE), jnp.float32),
        ],
        name="product_sums",
    )(left_lists, right_lists, sink_lists, counts, left_all, right_all)


def per_device(rows, cols, left_blocks, right_blocks, left_slots, right_slots, sink_slots, live_counts):
    right = right_blocks.reshape(RIGHT_ROWS, 2 * TILE_SIDE)
    left = left_blocks.reshape(LEFT_ROWS, 2 * TILE_SIDE)
    left_all, right_all = exchange(rows, cols, left, right)
    total = product_sums(
        left_slots.reshape(PANELS, PRODUCTS), right_slots.reshape(PANELS, PRODUCTS),
        sink_slots.reshape(PANELS, PRODUCTS), live_counts.reshape(PANELS), left_all, right_all)
    return total.reshape(1, 1, SINK_SLOTS, TILE_SIDE * TILE_SIDE)


def solution(mesh):
    return jax.shard_map(
        functools.partial(per_device, mesh.shape["row"], mesh.shape["col"]),
        mesh=mesh,
        in_specs=(
            P("row", "col", None, None),
            P("row", "col", None, None),
            P("row", "col", None, None, None),
            P("row", "col", None, None, None),
            P("row", "col", None, None, None),
            P("row", "col", None, None),
        ),
        out_specs=P("row", "col", None, None),
        check_vma=False,
    )
```

```python
import functools

import jax
import jax.numpy as jnp
from jax import lax
from jax.experimental import pallas as pl
from jax.experimental.pallas import tpu as pltpu
from jax.sharding import PartitionSpec as P

TILE_SIDE = 64
LEFT_SLOTS = 4
RIGHT_SLOTS = 20
SINK_SLOTS = 12
PRODUCTS = 24
SECTIONS = 4
PANELS = 2 * SECTIONS
CHUNKS = 4
LEFT_ROWS = LEFT_SLOTS * TILE_SIDE
RIGHT_ROWS = RIGHT_SLOTS * TILE_SIDE // 2
CHUNK_ROWS = RIGHT_ROWS // CHUNKS
TURNED = CHUNKS // 2
MESH = pl.DeviceIdType.MESH


def chosen(column, values):
    total = 0
    for place, value in enumerate(values):
        if value:
            total = total + (column % len(values) == place).astype(jnp.int32) * value
    return total


def exchange_kernel(rows, cols, left_ref, right_ref, left_all, right_all, relay,
                    left_send, left_recv, entry_send, right_recv, down_send, up_send,
                    relay_send, relay_recv):
    row = lax.axis_index("row")
    column = lax.axis_index("col")
    parity = row % 2
    half_row = row // 2
    below = (row + rows - 1) % rows
    above = (row + 1) % rows
    offset = chosen(column, (0, 0, 0, 6, 6, 6, 4, 2))
    turned_offset = chosen(column, (0, 6, 0, 6, 0, 6, 4, 2))
    relay_shift = chosen(column, (0, rows - 4, 0, 0, 4, 0, 0, 0))
    relays = relay_shift != 0
    shift = (2 * column + offset) % rows
    final_shift = (2 * column + turned_offset + rows - relay_shift) % rows
    moves = shift != 0
    greets_final = relays & (final_shift != relay_shift)

    def greet(row_to, column_to):
        pl.semaphore_signal(barrier, inc=1, device_id=(row_to, column_to), device_id_type=MESH)

    barrier = pltpu.get_barrier_semaphore()
    greet(below, column)
    greet(above, column)

    @pl.when(moves)
    def _():
        greet((row + shift) % rows, column)

    @pl.when(relays)
    def _():
        greet((row + relay_shift) % rows, column)

    @pl.when(greets_final)
    def _():
        greet((row + final_shift) % rows, column)

    for section in range(SECTIONS):
        @pl.when((half_row + section) % cols != 0)
        def _():
            greet(row, (column + half_row + section) % cols)

    peers = 2 + moves.astype(jnp.int32) + relays.astype(jnp.int32) + greets_final.astype(jnp.int32)
    for section in range(SECTIONS):
        peers += ((half_row + section) % cols != 0).astype(jnp.int32)
    pl.semaphore_wait(barrier, peers)

    def entry_of(chunk):
        if isinstance(chunk, int):
            return parity + (turned_offset if chunk < TURNED else offset)
        return parity + offset + (chunk < TURNED).astype(jnp.int32) * (turned_offset - offset)

    def part(chunk):
        return pl.ds(pl.multiple_of(chunk * CHUNK_ROWS, 8), CHUNK_ROWS)

    def entry_copy(chunk):
        return pltpu.make_async_remote_copy(
            src_ref=right_ref.at[part(chunk)], dst_ref=right_all.at[entry_of(chunk), part(chunk)],
            send_sem=entry_send.at[chunk], recv_sem=right_recv.at[entry_of(chunk), chunk],
            device_id=((row + rows - shift) % rows, column), device_id_type=MESH)

    def local_copy(chunk):
        return pltpu.make_async_copy(
            right_ref.at[part(chunk)], right_all.at[entry_of(chunk), part(chunk)],
            right_recv.at[entry_of(chunk), chunk])

    def relay_copy(chunk):
        return pltpu.make_async_remote_copy(
            src_ref=right_ref.at[part(chunk)], dst_ref=relay.at[part(chunk)],
            send_sem=entry_send.at[chunk], recv_sem=relay_recv.at[chunk],
            device_id=((row + rows - relay_shift) % rows, column), device_id_type=MESH)

    def final_copy(chunk):
        return pltpu.make_async_remote_copy(
            src_ref=relay.at[part(chunk)], dst_ref=right_all.at[entry_of(chunk), part(chunk)],
            send_sem=relay_send.at[chunk], recv_sem=right_recv.at[entry_of(chunk), chunk],
            device_id=((row + rows - final_shift) % rows, column), device_id_type=MESH)

    def left_copy(section):
        target = (column + 2 * cols - half_row - section) % cols
        return pltpu.make_async_remote_copy(
            src_ref=left_ref, dst_ref=left_all.at[section],
            send_sem=left_send.at[section], recv_sem=left_recv.at[section],
            device_id=(row, target), device_id_type=MESH)

    def left_local(section):
        return pltpu.make_async_copy(left_ref, left_all.at[section], left_recv.at[section])

    def down_copy(slot, chunk):
        return pltpu.make_async_remote_copy(
            src_ref=right_all.at[slot, part(chunk)],
            dst_ref=right_all.at[slot + 2 * (1 - parity), part(chunk)],
            send_sem=down_send.at[slot, chunk],
            recv_sem=right_recv.at[slot + 2 * (1 - parity), chunk],
            device_id=(below, column), device_id_type=MESH)

    def up_copy(slot, chunk):
        return pltpu.make_async_remote_copy(
            src_ref=right_all.at[slot, part(chunk)],
            dst_ref=right_all.at[slot - 2 * parity, part(chunk)],
            send_sem=up_send.at[slot, chunk],
            recv_sem=right_recv.at[slot - 2 * parity, chunk],
            device_id=(above, column), device_id_type=MESH)

    for chunk in range(CHUNKS):
        direct = moves if chunk >= TURNED else moves & jnp.logical_not(relays)

        @pl.when(direct)
        def _():
            entry_copy(chunk).start()

        @pl.when(jnp.logical_not(moves))
        def _():
            local_copy(chunk).start()

        if chunk < TURNED:
            @pl.when(relays)
            def _():
                relay_copy(chunk).start()

    for section in range(SECTIONS):
        @pl.when((half_row + section) % cols != 0)
        def _():
            left_copy(section).start()

        @pl.when((half_row + section) % cols == 0)
        def _():
            left_local(section).start()

    last_down = PANELS - 1 - 2 * (1 - parity)
    last_up = 2 * parity

    def arrived(slot, chunk):
        pltpu.make_async_copy(
            right_ref.at[part(chunk)], right_all.at[slot, part(chunk)], right_recv.at[slot, chunk]).wait()

    def first(chunk, carry):
        entry = entry_of(chunk)
        arrived(entry, chunk)

        @pl.when(entry <= last_down)
        def _():
            down_copy(entry, chunk).start()

        @pl.when(entry >= last_up)
        def _():
            up_copy(entry, chunk).start()
        return carry

    lax.fori_loop(TURNED, CHUNKS, first, 0)

    @pl.when(relays)
    def _():
        for chunk in range(TURNED):
            relay_copy(chunk).wait_recv()
            final_copy(chunk).start()

    lax.fori_loop(0, TURNED, first, 0)

    def onward(step, carry):
        distance = step // CHUNKS + 1
        chunk = (step + TURNED) % CHUNKS
        higher = entry_of(chunk) + distance
        lower = entry_of(chunk) - distance

        @pl.when(higher < PANELS)
        def _():
            arrived(higher, chunk)

        @pl.when(higher <= last_down)
        def _():
            down_copy(higher, chunk).start()

        @pl.when(lower >= 0)
        def _():
            arrived(lower, chunk)

        @pl.when(lower >= last_up)
        def _():
            up_copy(lower, chunk).start()
        return carry

    lax.fori_loop(0, (PANELS - 1) * CHUNKS, onward, 0)

    def sent(step, carry):
        slot = step // CHUNKS
        chunk = step % CHUNKS
        entry = entry_of(chunk)

        @pl.when((slot >= entry) & (slot <= last_down))
        def _():
            down_copy(slot, chunk).wait_send()

        @pl.when((slot <= entry) & (slot >= last_up))
        def _():
            up_copy(slot, chunk).wait_send()
        return carry

    lax.fori_loop(0, PANELS * CHUNKS, sent, 0)

    for chunk in range(CHUNKS):
        @pl.when(moves)
        def _():
            entry_copy(chunk).wait_send()

        if chunk < TURNED:
            @pl.when(relays)
            def _():
                final_copy(chunk).wait_send()

    for section in range(SECTIONS):
        @pl.when((half_row + section) % cols != 0)
        def _():
            left_copy(section).wait()

        @pl.when((half_row + section) % cols == 0)
        def _():
            left_local(section).wait()


def exchange(rows, cols, left, right):
    dma = pltpu.SemaphoreType.DMA
    return pl.pallas_call(
        functools.partial(exchange_kernel, rows, cols),
        out_shape=(
            jax.ShapeDtypeStruct((SECTIONS, LEFT_ROWS, 2 * TILE_SIDE), jnp.float32),
            jax.ShapeDtypeStruct((PANELS, RIGHT_ROWS, 2 * TILE_SIDE), jnp.float32),
        ),
        in_specs=[pl.BlockSpec(memory_space=pltpu.VMEM)] * 2,
        out_specs=(pl.BlockSpec(memory_space=pltpu.VMEM),) * 2,
        scratch_shapes=[
            pltpu.VMEM((TURNED * CHUNK_ROWS, 2 * TILE_SIDE), jnp.float32),
            dma((SECTIONS,)), dma((SECTIONS,)), dma((CHUNKS,)), dma((PANELS, CHUNKS)),
            dma((PANELS, CHUNKS)), dma((PANELS, CHUNKS)), dma((TURNED,)), dma((TURNED,)),
        ],
        compiler_params=pltpu.CompilerParams(collective_id=0, has_side_effects=True),
        name="exchange",
    )(left, right)


def product_kernel(left_lists, right_lists, sink_lists, counts, left_all, right_all, out, products, sums):
    side = TILE_SIDE
    section = pl.program_id(0)

    @pl.when(section == 0)
    def _():
        sums[...] = jnp.zeros_like(sums)

    def ordered(count):
        return lax.broadcasted_iota(jnp.int32, (count, 2 * side), 1) < side

    place = lax.broadcasted_iota(jnp.int32, (2 * side, 2 * side), 0)
    target = lax.broadcasted_iota(jnp.int32, (2 * side, 2 * side), 1)
    moved = (place & side) + (place & 1) * (side // 2) + ((place & (side - 1)) >> 1)
    evens_first = (moved == target).astype(jnp.float32).astype(jnp.bfloat16)
    rows = LEFT_ROWS // 2
    low_lanes, low_lanes_left = ordered(side // 2), ordered(rows)
    for half in range(2):
        left = jnp.concatenate(
            [left_all[0, pl.ds(half * rows + slot, side // 2, stride=LEFT_SLOTS), :] for slot in range(LEFT_SLOTS)],
            axis=0)
        turned = pltpu.roll(left, side, 1)
        even = jnp.where(low_lanes_left, left, turned).reshape(LEFT_SLOTS, side // 2, 2 * side)
        odd = jnp.where(low_lanes_left, turned, left).reshape(LEFT_SLOTS, side // 2, 2 * side)
        twice = jnp.concatenate([even, odd], axis=1).reshape(LEFT_ROWS, 2 * side)
        high = twice.astype(jnp.bfloat16).astype(jnp.float32)
        split = jnp.where(ordered(LEFT_ROWS), high, twice - high).astype(jnp.bfloat16)
        split = jnp.dot(split, evens_first, preferred_element_type=jnp.float32).astype(jnp.bfloat16)
        stream = jnp.concatenate([split, split], axis=1)
        item = 2 * section + half
        for quad in range(RIGHT_SLOTS // 4):
            pairs = []
            for pair in range(2):
                base = (4 * quad + 2 * pair) * (side // 2)
                first = right_all[half, pl.ds(base, side // 2), :]
                second = right_all[half, pl.ds(base + side // 2, side // 2), :]
                pairs.append(jnp.concatenate([
                    jnp.where(low_lanes, first, pltpu.roll(second, side, 1)),
                    jnp.where(low_lanes, pltpu.roll(first, side, 1), second)], axis=0))
            right = jnp.concatenate(pairs, axis=1)
            right_high = right.astype(jnp.bfloat16)
            right_low = (right - right_high.astype(jnp.float32)).astype(jnp.bfloat16)
            held = jnp.concatenate([right_high, right_high, right_low, right_low], axis=0)
            found = jnp.dot(stream, held, preferred_element_type=jnp.float32)
            for n in range(2):
                products[pl.ds(LEFT_SLOTS * (2 * quad + n), LEFT_SLOTS)] = (
                    found[:, 2 * side * n : 2 * side * (n + 1)].reshape(LEFT_SLOTS, side, 2 * side))

        def listed(position):
            right_slot = right_lists[item, position]
            source = LEFT_SLOTS * (right_slot >> 1) + left_lists[item, position]
            return source, 2 * sink_lists[item, position] + (right_slot & 1)

        def add(position, ahead):
            source, sink = ahead
            following = listed(jnp.minimum(position + 1, PRODUCTS - 1))
            sums[sink] += products[source]
            return following

        lax.fori_loop(0, counts[item], add, listed(0))

    @pl.when(section == SECTIONS - 1)
    def _():
        for sink in range(SINK_SLOTS):
            total = sums[2 * sink] + pltpu.roll(sums[2 * sink + 1], side, 1)
            out[pl.ds(sink * (side // 2), side // 2), :] = jnp.where(
                low_lanes, total[: side // 2], pltpu.roll(total[side // 2 :], side, 1))


def product_sums(left_lists, right_lists, sink_lists, counts, left_all, right_all):
    smem = pl.BlockSpec(memory_space=pltpu.SMEM)
    return pl.pallas_call(
        product_kernel,
        out_shape=jax.ShapeDtypeStruct((SINK_SLOTS * TILE_SIDE // 2, 2 * TILE_SIDE), jnp.float32),
        grid=(SECTIONS,),
        in_specs=[smem] * 4 + [
            pl.BlockSpec((1, LEFT_ROWS, 2 * TILE_SIDE), lambda section: (section, 0, 0)),
            pl.BlockSpec((2, RIGHT_ROWS, 2 * TILE_SIDE), lambda section: (section, 0, 0)),
        ],
        out_specs=pl.BlockSpec((SINK_SLOTS * TILE_SIDE // 2, 2 * TILE_SIDE), lambda section: (0, 0)),
        scratch_shapes=[
            pltpu.VMEM((LEFT_SLOTS * RIGHT_SLOTS // 2, TILE_SIDE, 2 * TILE_SIDE), jnp.float32),
            pltpu.VMEM((2 * SINK_SLOTS, TILE_SIDE, 2 * TILE_SIDE), jnp.float32),
        ],
        name="product_sums",
    )(left_lists, right_lists, sink_lists, counts, left_all, right_all)


def per_device(rows, cols, left_blocks, right_blocks, left_slots, right_slots, sink_slots, live_counts):
    right = right_blocks.reshape(RIGHT_ROWS, 2 * TILE_SIDE)
    left = left_blocks.reshape(2, LEFT_SLOTS, TILE_SIDE // 2, 2 * TILE_SIDE).transpose(0, 2, 1, 3).reshape(LEFT_ROWS, 2 * TILE_SIDE)
    left_all, right_all = exchange(rows, cols, left, right)
    total = product_sums(
        left_slots.reshape(PANELS, PRODUCTS), right_slots.reshape(PANELS, PRODUCTS),
        sink_slots.reshape(PANELS, PRODUCTS), live_counts.reshape(PANELS), left_all, right_all)
    return total.reshape(1, 1, SINK_SLOTS, TILE_SIDE * TILE_SIDE)


def solution(mesh):
    return jax.shard_map(
        functools.partial(per_device, mesh.shape["row"], mesh.shape["col"]),
        mesh=mesh,
        in_specs=(
            P("row", "col", None, None),
            P("row", "col", None, None),
            P("row", "col", None, None, None),
            P("row", "col", None, None, None),
            P("row", "col", None, None, None),
            P("row", "col", None, None),
        ),
        out_specs=P("row", "col", None, None),
        check_vma=False,
    )
```

```python
import functools

import jax
import jax.numpy as jnp
from jax import lax
from jax.experimental import pallas as pl
from jax.experimental.pallas import tpu as pltpu
from jax.sharding import PartitionSpec as P

TILE_SIDE = 64
LEFT_SLOTS = 4
RIGHT_SLOTS = 20
SINK_SLOTS = 12
PRODUCTS = 24
SECTIONS = 4
PANELS = 2 * SECTIONS
CHUNKS = 4
LEFT_ROWS = LEFT_SLOTS * TILE_SIDE
RIGHT_ROWS = RIGHT_SLOTS * TILE_SIDE // 2
CHUNK_ROWS = RIGHT_ROWS // CHUNKS
TURNED = CHUNKS // 2
MESH = pl.DeviceIdType.MESH


def chosen(column, values):
    total = 0
    for place, value in enumerate(values):
        if value:
            total = total + (column % len(values) == place).astype(jnp.int32) * value
    return total


def exchange_kernel(rows, cols, left_ref, right_ref, left_all, right_all, relay,
                    left_send, left_recv, entry_send, right_recv, down_send, up_send,
                    relay_send, relay_recv):
    row = lax.axis_index("row")
    column = lax.axis_index("col")
    parity = row % 2
    half_row = row // 2
    below = (row + rows - 1) % rows
    above = (row + 1) % rows
    offset = chosen(column, (0, 4, 0, 6, 2, 6, 2, 4))
    turned_offset = chosen(column, (0, 6, 0, 6, 0, 6, 2, 4))
    relay_shift = chosen(column, (0, rows - 4, 0, 0, 4, 0, 0, 0))
    relays = relay_shift != 0
    shift = (2 * column + offset) % rows
    final_shift = (2 * column + turned_offset + rows - relay_shift) % rows
    moves = shift != 0
    greets_final = relays & (final_shift != relay_shift)

    def greet(row_to, column_to):
        pl.semaphore_signal(barrier, inc=1, device_id=(row_to, column_to), device_id_type=MESH)

    barrier = pltpu.get_barrier_semaphore()
    greet(below, column)
    greet(above, column)

    @pl.when(moves)
    def _():
        greet((row + shift) % rows, column)

    @pl.when(relays)
    def _():
        greet((row + relay_shift) % rows, column)

    @pl.when(greets_final)
    def _():
        greet((row + final_shift) % rows, column)

    for section in range(SECTIONS):
        @pl.when((half_row + section) % cols != 0)
        def _():
            greet(row, (column + half_row + section) % cols)

    peers = 2 + moves.astype(jnp.int32) + relays.astype(jnp.int32) + greets_final.astype(jnp.int32)
    for section in range(SECTIONS):
        peers += ((half_row + section) % cols != 0).astype(jnp.int32)
    pl.semaphore_wait(barrier, peers)

    def entry_of(chunk):
        if isinstance(chunk, int):
            return parity + (turned_offset if chunk < TURNED else offset)
        return parity + offset + (chunk < TURNED).astype(jnp.int32) * (turned_offset - offset)

    def part(chunk):
        return pl.ds(pl.multiple_of(chunk * CHUNK_ROWS, 8), CHUNK_ROWS)

    def entry_copy(chunk):
        return pltpu.make_async_remote_copy(
            src_ref=right_ref.at[part(chunk)], dst_ref=right_all.at[entry_of(chunk), part(chunk)],
            send_sem=entry_send.at[chunk], recv_sem=right_recv.at[entry_of(chunk), chunk],
            device_id=((row + rows - shift) % rows, column), device_id_type=MESH)

    def local_copy(chunk):
        return pltpu.make_async_copy(
            right_ref.at[part(chunk)], right_all.at[entry_of(chunk), part(chunk)],
            right_recv.at[entry_of(chunk), chunk])

    def relay_copy(chunk):
        return pltpu.make_async_remote_copy(
            src_ref=right_ref.at[part(chunk)], dst_ref=relay.at[part(chunk)],
            send_sem=entry_send.at[chunk], recv_sem=relay_recv.at[chunk],
            device_id=((row + rows - relay_shift) % rows, column), device_id_type=MESH)

    def final_copy(chunk):
        return pltpu.make_async_remote_copy(
            src_ref=relay.at[part(chunk)], dst_ref=right_all.at[entry_of(chunk), part(chunk)],
            send_sem=relay_send.at[chunk], recv_sem=right_recv.at[entry_of(chunk), chunk],
            device_id=((row + rows - final_shift) % rows, column), device_id_type=MESH)

    def left_copy(section):
        target = (column + 2 * cols - half_row - section) % cols
        return pltpu.make_async_remote_copy(
            src_ref=left_ref, dst_ref=left_all.at[section],
            send_sem=left_send.at[section], recv_sem=left_recv.at[section],
            device_id=(row, target), device_id_type=MESH)

    def left_local(section):
        return pltpu.make_async_copy(left_ref, left_all.at[section], left_recv.at[section])

    def down_copy(slot, chunk):
        return pltpu.make_async_remote_copy(
            src_ref=right_all.at[slot, part(chunk)],
            dst_ref=right_all.at[slot + 2 * (1 - parity), part(chunk)],
            send_sem=down_send.at[slot, chunk],
            recv_sem=right_recv.at[slot + 2 * (1 - parity), chunk],
            device_id=(below, column), device_id_type=MESH)

    def up_copy(slot, chunk):
        return pltpu.make_async_remote_copy(
            src_ref=right_all.at[slot, part(chunk)],
            dst_ref=right_all.at[slot - 2 * parity, part(chunk)],
            send_sem=up_send.at[slot, chunk],
            recv_sem=right_recv.at[slot - 2 * parity, chunk],
            device_id=(above, column), device_id_type=MESH)

    for chunk in range(CHUNKS):
        direct = moves if chunk >= TURNED else moves & jnp.logical_not(relays)

        @pl.when(direct)
        def _():
            entry_copy(chunk).start()

        @pl.when(jnp.logical_not(moves))
        def _():
            local_copy(chunk).start()

        if chunk < TURNED:
            @pl.when(relays)
            def _():
                relay_copy(chunk).start()

    for section in range(SECTIONS):
        @pl.when((half_row + section) % cols != 0)
        def _():
            left_copy(section).start()

        @pl.when((half_row + section) % cols == 0)
        def _():
            left_local(section).start()

    last_down = PANELS - 1 - 2 * (1 - parity)
    last_up = 2 * parity

    def arrived(slot, chunk):
        pltpu.make_async_copy(
            right_ref.at[part(chunk)], right_all.at[slot, part(chunk)], right_recv.at[slot, chunk]).wait()

    def first(chunk, carry):
        entry = entry_of(chunk)
        arrived(entry, chunk)

        @pl.when(entry <= last_down)
        def _():
            down_copy(entry, chunk).start()

        @pl.when(entry >= last_up)
        def _():
            up_copy(entry, chunk).start()
        return carry

    lax.fori_loop(TURNED, CHUNKS, first, 0)

    @pl.when(relays)
    def _():
        for chunk in range(TURNED):
            relay_copy(chunk).wait_recv()
            final_copy(chunk).start()

    lax.fori_loop(0, TURNED, first, 0)

    def onward(step, carry):
        distance = step // CHUNKS + 1
        chunk = (step + TURNED) % CHUNKS
        higher = entry_of(chunk) + distance
        lower = entry_of(chunk) - distance

        @pl.when(higher < PANELS)
        def _():
            arrived(higher, chunk)

        @pl.when(higher <= last_down)
        def _():
            down_copy(higher, chunk).start()

        @pl.when(lower >= 0)
        def _():
            arrived(lower, chunk)

        @pl.when(lower >= last_up)
        def _():
            up_copy(lower, chunk).start()
        return carry

    lax.fori_loop(0, (PANELS - 1) * CHUNKS, onward, 0)

    def sent(step, carry):
        slot = step // CHUNKS
        chunk = step % CHUNKS
        entry = entry_of(chunk)

        @pl.when((slot >= entry) & (slot <= last_down))
        def _():
            down_copy(slot, chunk).wait_send()

        @pl.when((slot <= entry) & (slot >= last_up))
        def _():
            up_copy(slot, chunk).wait_send()
        return carry

    lax.fori_loop(0, PANELS * CHUNKS, sent, 0)

    for chunk in range(CHUNKS):
        @pl.when(moves)
        def _():
            entry_copy(chunk).wait_send()

        if chunk < TURNED:
            @pl.when(relays)
            def _():
                final_copy(chunk).wait_send()

    for section in range(SECTIONS):
        @pl.when((half_row + section) % cols != 0)
        def _():
            left_copy(section).wait()

        @pl.when((half_row + section) % cols == 0)
        def _():
            left_local(section).wait()


def exchange(rows, cols, left, right):
    dma = pltpu.SemaphoreType.DMA
    return pl.pallas_call(
        functools.partial(exchange_kernel, rows, cols),
        out_shape=(
            jax.ShapeDtypeStruct((SECTIONS, LEFT_ROWS, 2 * TILE_SIDE), jnp.float32),
            jax.ShapeDtypeStruct((PANELS, RIGHT_ROWS, 2 * TILE_SIDE), jnp.float32),
        ),
        in_specs=[pl.BlockSpec(memory_space=pltpu.VMEM)] * 2,
        out_specs=(pl.BlockSpec(memory_space=pltpu.VMEM),) * 2,
        scratch_shapes=[
            pltpu.VMEM((TURNED * CHUNK_ROWS, 2 * TILE_SIDE), jnp.float32),
            dma((SECTIONS,)), dma((SECTIONS,)), dma((CHUNKS,)), dma((PANELS, CHUNKS)),
            dma((PANELS, CHUNKS)), dma((PANELS, CHUNKS)), dma((TURNED,)), dma((TURNED,)),
        ],
        compiler_params=pltpu.CompilerParams(collective_id=0, has_side_effects=True),
        name="exchange",
    )(left, right)


def product_kernel(left_lists, right_lists, sink_lists, counts, left_all, right_all, out, products, sums):
    side = TILE_SIDE
    section = pl.program_id(0)

    @pl.when(section == 0)
    def _():
        sums[...] = jnp.zeros_like(sums)

    def ordered(count):
        return lax.broadcasted_iota(jnp.int32, (count, 2 * side), 1) < side

    place = lax.broadcasted_iota(jnp.int32, (2 * side, 2 * side), 0)
    target = lax.broadcasted_iota(jnp.int32, (2 * side, 2 * side), 1)
    moved = (place & side) + (place & 1) * (side // 2) + ((place & (side - 1)) >> 1)
    evens_first = (moved == target).astype(jnp.float32).astype(jnp.bfloat16)
    rows = LEFT_ROWS // 2
    low_lanes, low_lanes_left = ordered(side // 2), ordered(rows)
    for half in range(2):
        left = jnp.concatenate(
            [left_all[0, pl.ds(half * rows + slot, side // 2, stride=LEFT_SLOTS), :] for slot in range(LEFT_SLOTS)],
            axis=0)
        turned = pltpu.roll(left, side, 1)
        even = jnp.where(low_lanes_left, left, turned).reshape(LEFT_SLOTS, side // 2, 2 * side)
        odd = jnp.where(low_lanes_left, turned, left).reshape(LEFT_SLOTS, side // 2, 2 * side)
        twice = jnp.concatenate([even, odd], axis=1).reshape(LEFT_ROWS, 2 * side)
        high = twice.astype(jnp.bfloat16).astype(jnp.float32)
        split = jnp.where(ordered(LEFT_ROWS), high, twice - high).astype(jnp.bfloat16)
        split = jnp.dot(split, evens_first, preferred_element_type=jnp.float32).astype(jnp.bfloat16)
        stream = jnp.concatenate([split, split], axis=1)
        item = 2 * section + half
        for quad in range(RIGHT_SLOTS // 4):
            pairs = []
            for pair in range(2):
                base = (4 * quad + 2 * pair) * (side // 2)
                first = right_all[half, pl.ds(base, side // 2), :]
                second = right_all[half, pl.ds(base + side // 2, side // 2), :]
                pairs.append(jnp.concatenate([
                    jnp.where(low_lanes, first, pltpu.roll(second, side, 1)),
                    jnp.where(low_lanes, pltpu.roll(first, side, 1), second)], axis=0))
            right = jnp.concatenate(pairs, axis=1)
            right_high = right.astype(jnp.bfloat16)
            right_low = (right - right_high.astype(jnp.float32)).astype(jnp.bfloat16)
            held = jnp.concatenate([right_high, right_high, right_low, right_low], axis=0)
            found = jnp.dot(stream, held, preferred_element_type=jnp.float32)
            for n in range(2):
                products[pl.ds(LEFT_SLOTS * (2 * quad + n), LEFT_SLOTS)] = (
                    found[:, 2 * side * n : 2 * side * (n + 1)].reshape(LEFT_SLOTS, side, 2 * side))

        def listed(position):
            right_slot = right_lists[item, position]
            source = LEFT_SLOTS * (right_slot >> 1) + left_lists[item, position]
            return source, 2 * sink_lists[item, position] + (right_slot & 1)

        def add(position, ahead):
            source, sink = ahead
            following = listed(jnp.minimum(position + 1, PRODUCTS - 1))
            sums[sink] += products[source]
            return following

        lax.fori_loop(0, counts[item], add, listed(0))

    @pl.when(section == SECTIONS - 1)
    def _():
        for sink in range(SINK_SLOTS):
            total = sums[2 * sink] + pltpu.roll(sums[2 * sink + 1], side, 1)
            out[pl.ds(sink * (side // 2), side // 2), :] = jnp.where(
                low_lanes, total[: side // 2], pltpu.roll(total[side // 2 :], side, 1))


def product_sums(left_lists, right_lists, sink_lists, counts, left_all, right_all):
    smem = pl.BlockSpec(memory_space=pltpu.SMEM)
    return pl.pallas_call(
        product_kernel,
        out_shape=jax.ShapeDtypeStruct((SINK_SLOTS * TILE_SIDE // 2, 2 * TILE_SIDE), jnp.float32),
        grid=(SECTIONS,),
        in_specs=[smem] * 4 + [
            pl.BlockSpec((1, LEFT_ROWS, 2 * TILE_SIDE), lambda section: (section, 0, 0)),
            pl.BlockSpec((2, RIGHT_ROWS, 2 * TILE_SIDE), lambda section: (section, 0, 0)),
        ],
        out_specs=pl.BlockSpec((SINK_SLOTS * TILE_SIDE // 2, 2 * TILE_SIDE), lambda section: (0, 0)),
        scratch_shapes=[
            pltpu.VMEM((LEFT_SLOTS * RIGHT_SLOTS // 2, TILE_SIDE, 2 * TILE_SIDE), jnp.float32),
            pltpu.VMEM((2 * SINK_SLOTS, TILE_SIDE, 2 * TILE_SIDE), jnp.float32),
        ],
        name="product_sums",
    )(left_lists, right_lists, sink_lists, counts, left_all, right_all)


def per_device(rows, cols, left_blocks, right_blocks, left_slots, right_slots, sink_slots, live_counts):
    right = right_blocks.reshape(RIGHT_ROWS, 2 * TILE_SIDE)
    left = left_blocks.reshape(2, LEFT_SLOTS, TILE_SIDE // 2, 2 * TILE_SIDE).transpose(0, 2, 1, 3).reshape(LEFT_ROWS, 2 * TILE_SIDE)
    left_all, right_all = exchange(rows, cols, left, right)
    total = product_sums(
        left_slots.reshape(PANELS, PRODUCTS), right_slots.reshape(PANELS, PRODUCTS),
        sink_slots.reshape(PANELS, PRODUCTS), live_counts.reshape(PANELS), left_all, right_all)
    return total.reshape(1, 1, SINK_SLOTS, TILE_SIDE * TILE_SIDE)


def solution(mesh):
    return jax.shard_map(
        functools.partial(per_device, mesh.shape["row"], mesh.shape["col"]),
        mesh=mesh,
        in_specs=(
            P("row", "col", None, None),
            P("row", "col", None, None),
            P("row", "col", None, None, None),
            P("row", "col", None, None, None),
            P("row", "col", None, None, None),
            P("row", "col", None, None),
        ),
        out_specs=P("row", "col", None, None),
        check_vma=False,
    )
```

```python
import functools

import jax
import jax.numpy as jnp
from jax import lax
from jax.experimental import pallas as pl
from jax.experimental.pallas import tpu as pltpu
from jax.sharding import PartitionSpec as P

TILE_SIDE = 64
LEFT_SLOTS = 4
RIGHT_SLOTS = 20
SINK_SLOTS = 12
PRODUCTS = 24
SECTIONS = 4
PANELS = 2 * SECTIONS
CHUNKS = 4
LEFT_ROWS = LEFT_SLOTS * TILE_SIDE
RIGHT_ROWS = RIGHT_SLOTS * TILE_SIDE // 2
CHUNK_ROWS = RIGHT_ROWS // CHUNKS
TURNED = CHUNKS // 4
MESH = pl.DeviceIdType.MESH


def chosen(column, values):
    total = 0
    for place, value in enumerate(values):
        if value:
            total = total + (column % len(values) == place).astype(jnp.int32) * value
    return total


def exchange_kernel(rows, cols, left_ref, right_ref, left_all, right_all, relay,
                    left_send, left_recv, entry_send, right_recv, down_send, up_send,
                    relay_send, relay_recv):
    row = lax.axis_index("row")
    column = lax.axis_index("col")
    parity = row % 2
    half_row = row // 2
    below = (row + rows - 1) % rows
    above = (row + 1) % rows
    offset = chosen(column, (0, 4, 0, 6, 2, 6, 2, 4))
    turned_offset = chosen(column, (0, 6, 0, 6, 0, 6, 2, 4))
    relay_shift = chosen(column, (0, rows - 4, 0, 0, 4, 0, 0, 0))
    relays = relay_shift != 0
    shift = (2 * column + offset) % rows
    final_shift = (2 * column + turned_offset + rows - relay_shift) % rows
    moves = shift != 0
    greets_final = relays & (final_shift != relay_shift)

    def greet(row_to, column_to):
        pl.semaphore_signal(barrier, inc=1, device_id=(row_to, column_to), device_id_type=MESH)

    barrier = pltpu.get_barrier_semaphore()
    greet(below, column)
    greet(above, column)

    @pl.when(moves)
    def _():
        greet((row + shift) % rows, column)

    @pl.when(relays)
    def _():
        greet((row + relay_shift) % rows, column)

    @pl.when(greets_final)
    def _():
        greet((row + final_shift) % rows, column)

    for section in range(SECTIONS):
        @pl.when((half_row + section) % cols != 0)
        def _():
            greet(row, (column + half_row + section) % cols)

    peers = 2 + moves.astype(jnp.int32) + relays.astype(jnp.int32) + greets_final.astype(jnp.int32)
    for section in range(SECTIONS):
        peers += ((half_row + section) % cols != 0).astype(jnp.int32)
    pl.semaphore_wait(barrier, peers)

    def entry_of(chunk):
        if isinstance(chunk, int):
            return parity + (turned_offset if chunk < TURNED else offset)
        return parity + offset + (chunk < TURNED).astype(jnp.int32) * (turned_offset - offset)

    def part(chunk):
        return pl.ds(pl.multiple_of(chunk * CHUNK_ROWS, 8), CHUNK_ROWS)

    def entry_copy(chunk):
        return pltpu.make_async_remote_copy(
            src_ref=right_ref.at[part(chunk)], dst_ref=right_all.at[entry_of(chunk), part(chunk)],
            send_sem=entry_send.at[chunk], recv_sem=right_recv.at[entry_of(chunk), chunk],
            device_id=((row + rows - shift) % rows, column), device_id_type=MESH)

    def local_copy(chunk):
        return pltpu.make_async_copy(
            right_ref.at[part(chunk)], right_all.at[entry_of(chunk), part(chunk)],
            right_recv.at[entry_of(chunk), chunk])

    def relay_copy(chunk):
        return pltpu.make_async_remote_copy(
            src_ref=right_ref.at[part(chunk)], dst_ref=relay.at[part(chunk)],
            send_sem=entry_send.at[chunk], recv_sem=relay_recv.at[chunk],
            device_id=((row + rows - relay_shift) % rows, column), device_id_type=MESH)

    def final_copy(chunk):
        return pltpu.make_async_remote_copy(
            src_ref=relay.at[part(chunk)], dst_ref=right_all.at[entry_of(chunk), part(chunk)],
            send_sem=relay_send.at[chunk], recv_sem=right_recv.at[entry_of(chunk), chunk],
            device_id=((row + rows - final_shift) % rows, column), device_id_type=MESH)

    def left_copy(section):
        target = (column + 2 * cols - half_row - section) % cols
        return pltpu.make_async_remote_copy(
            src_ref=left_ref, dst_ref=left_all.at[section],
            send_sem=left_send.at[section], recv_sem=left_recv.at[section],
            device_id=(row, target), device_id_type=MESH)

    def left_local(section):
        return pltpu.make_async_copy(left_ref, left_all.at[section], left_recv.at[section])

    def down_copy(slot, chunk):
        return pltpu.make_async_remote_copy(
            src_ref=right_all.at[slot, part(chunk)],
            dst_ref=right_all.at[slot + 2 * (1 - parity), part(chunk)],
            send_sem=down_send.at[slot, chunk],
            recv_sem=right_recv.at[slot + 2 * (1 - parity), chunk],
            device_id=(below, column), device_id_type=MESH)

    def up_copy(slot, chunk):
        return pltpu.make_async_remote_copy(
            src_ref=right_all.at[slot, part(chunk)],
            dst_ref=right_all.at[slot - 2 * parity, part(chunk)],
            send_sem=up_send.at[slot, chunk],
            recv_sem=right_recv.at[slot - 2 * parity, chunk],
            device_id=(above, column), device_id_type=MESH)

    for chunk in range(CHUNKS):
        direct = moves if chunk >= TURNED else moves & jnp.logical_not(relays)

        @pl.when(direct)
        def _():
            entry_copy(chunk).start()

        @pl.when(jnp.logical_not(moves))
        def _():
            local_copy(chunk).start()

        if chunk < TURNED:
            @pl.when(relays)
            def _():
                relay_copy(chunk).start()

    for section in range(SECTIONS):
        @pl.when((half_row + section) % cols != 0)
        def _():
            left_copy(section).start()

        @pl.when((half_row + section) % cols == 0)
        def _():
            left_local(section).start()

    last_down = PANELS - 1 - 2 * (1 - parity)
    last_up = 2 * parity

    def arrived(slot, chunk):
        pltpu.make_async_copy(
            right_ref.at[part(chunk)], right_all.at[slot, part(chunk)], right_recv.at[slot, chunk]).wait()

    def first(chunk, carry):
        entry = entry_of(chunk)
        arrived(entry, chunk)

        @pl.when(entry <= last_down)
        def _():
            down_copy(entry, chunk).start()

        @pl.when(entry >= last_up)
        def _():
            up_copy(entry, chunk).start()
        return carry

    lax.fori_loop(TURNED, CHUNKS, first, 0)

    @pl.when(relays)
    def _():
        for chunk in range(TURNED):
            relay_copy(chunk).wait_recv()
            final_copy(chunk).start()

    lax.fori_loop(0, TURNED, first, 0)

    def onward(step, carry):
        distance = step // CHUNKS + 1
        chunk = (step + TURNED) % CHUNKS
        higher = entry_of(chunk) + distance
        lower = entry_of(chunk) - distance

        @pl.when(higher < PANELS)
        def _():
            arrived(higher, chunk)

        @pl.when(higher <= last_down)
        def _():
            down_copy(higher, chunk).start()

        @pl.when(lower >= 0)
        def _():
            arrived(lower, chunk)

        @pl.when(lower >= last_up)
        def _():
            up_copy(lower, chunk).start()
        return carry

    lax.fori_loop(0, (PANELS - 1) * CHUNKS, onward, 0)

    def sent(step, carry):
        slot = step // CHUNKS
        chunk = step % CHUNKS
        entry = entry_of(chunk)

        @pl.when((slot >= entry) & (slot <= last_down))
        def _():
            down_copy(slot, chunk).wait_send()

        @pl.when((slot <= entry) & (slot >= last_up))
        def _():
            up_copy(slot, chunk).wait_send()
        return carry

    lax.fori_loop(0, PANELS * CHUNKS, sent, 0)

    for chunk in range(CHUNKS):
        @pl.when(moves)
        def _():
            entry_copy(chunk).wait_send()

        if chunk < TURNED:
            @pl.when(relays)
            def _():
                final_copy(chunk).wait_send()

    for section in range(SECTIONS):
        @pl.when((half_row + section) % cols != 0)
        def _():
            left_copy(section).wait()

        @pl.when((half_row + section) % cols == 0)
        def _():
            left_local(section).wait()


def exchange(rows, cols, left, right):
    dma = pltpu.SemaphoreType.DMA
    return pl.pallas_call(
        functools.partial(exchange_kernel, rows, cols),
        out_shape=(
            jax.ShapeDtypeStruct((SECTIONS, LEFT_ROWS, 2 * TILE_SIDE), jnp.float32),
            jax.ShapeDtypeStruct((PANELS, RIGHT_ROWS, 2 * TILE_SIDE), jnp.float32),
        ),
        in_specs=[pl.BlockSpec(memory_space=pltpu.VMEM)] * 2,
        out_specs=(pl.BlockSpec(memory_space=pltpu.VMEM),) * 2,
        scratch_shapes=[
            pltpu.VMEM((TURNED * CHUNK_ROWS, 2 * TILE_SIDE), jnp.float32),
            dma((SECTIONS,)), dma((SECTIONS,)), dma((CHUNKS,)), dma((PANELS, CHUNKS)),
            dma((PANELS, CHUNKS)), dma((PANELS, CHUNKS)), dma((TURNED,)), dma((TURNED,)),
        ],
        compiler_params=pltpu.CompilerParams(collective_id=0, has_side_effects=True),
        name="exchange",
    )(left, right)


def product_kernel(left_lists, right_lists, sink_lists, counts, left_all, right_all, out, products, sums):
    side = TILE_SIDE
    section = pl.program_id(0)

    @pl.when(section == 0)
    def _():
        sums[...] = jnp.zeros_like(sums)

    def ordered(count):
        return lax.broadcasted_iota(jnp.int32, (count, 2 * side), 1) < side

    place = lax.broadcasted_iota(jnp.int32, (2 * side, 2 * side), 0)
    target = lax.broadcasted_iota(jnp.int32, (2 * side, 2 * side), 1)
    moved = (place & side) + (place & 1) * (side // 2) + ((place & (side - 1)) >> 1)
    evens_first = (moved == target).astype(jnp.float32).astype(jnp.bfloat16)
    rows = LEFT_ROWS // 2
    low_lanes, low_lanes_left = ordered(side // 2), ordered(rows)
    for half in range(2):
        left = jnp.concatenate(
            [left_all[0, pl.ds(half * rows + slot, side // 2, stride=LEFT_SLOTS), :] for slot in range(LEFT_SLOTS)],
            axis=0)
        turned = pltpu.roll(left, side, 1)
        even = jnp.where(low_lanes_left, left, turned).reshape(LEFT_SLOTS, side // 2, 2 * side)
        odd = jnp.where(low_lanes_left, turned, left).reshape(LEFT_SLOTS, side // 2, 2 * side)
        twice = jnp.concatenate([even, odd], axis=1).reshape(LEFT_ROWS, 2 * side)
        high = twice.astype(jnp.bfloat16).astype(jnp.float32)
        split = jnp.where(ordered(LEFT_ROWS), high, twice - high).astype(jnp.bfloat16)
        split = jnp.dot(split, evens_first, preferred_element_type=jnp.float32).astype(jnp.bfloat16)
        stream = jnp.concatenate([split, split], axis=1)
        item = 2 * section + half
        for quad in range(RIGHT_SLOTS // 4):
            pairs = []
            for pair in range(2):
                base = (4 * quad + 2 * pair) * (side // 2)
                first = right_all[half, pl.ds(base, side // 2), :]
                second = right_all[half, pl.ds(base + side // 2, side // 2), :]
                pairs.append(jnp.concatenate([
                    jnp.where(low_lanes, first, pltpu.roll(second, side, 1)),
                    jnp.where(low_lanes, pltpu.roll(first, side, 1), second)], axis=0))
            right = jnp.concatenate(pairs, axis=1)
            right_high = right.astype(jnp.bfloat16)
            right_low = (right - right_high.astype(jnp.float32)).astype(jnp.bfloat16)
            held = jnp.concatenate([right_high, right_high, right_low, right_low], axis=0)
            found = jnp.dot(stream, held, preferred_element_type=jnp.float32)
            for n in range(2):
                products[pl.ds(LEFT_SLOTS * (2 * quad + n), LEFT_SLOTS)] = (
                    found[:, 2 * side * n : 2 * side * (n + 1)].reshape(LEFT_SLOTS, side, 2 * side))

        def listed(position):
            right_slot = right_lists[item, position]
            source = LEFT_SLOTS * (right_slot >> 1) + left_lists[item, position]
            return source, 2 * sink_lists[item, position] + (right_slot & 1)

        def add(position, ahead):
            source, sink = ahead
            following = listed(jnp.minimum(position + 1, PRODUCTS - 1))
            sums[sink] += products[source]
            return following

        lax.fori_loop(0, counts[item], add, listed(0))

    @pl.when(section == SECTIONS - 1)
    def _():
        for sink in range(SINK_SLOTS):
            total = sums[2 * sink] + pltpu.roll(sums[2 * sink + 1], side, 1)
            out[pl.ds(sink * (side // 2), side // 2), :] = jnp.where(
                low_lanes, total[: side // 2], pltpu.roll(total[side // 2 :], side, 1))


def product_sums(left_lists, right_lists, sink_lists, counts, left_all, right_all):
    smem = pl.BlockSpec(memory_space=pltpu.SMEM)
    return pl.pallas_call(
        product_kernel,
        out_shape=jax.ShapeDtypeStruct((SINK_SLOTS * TILE_SIDE // 2, 2 * TILE_SIDE), jnp.float32),
        grid=(SECTIONS,),
        in_specs=[smem] * 4 + [
            pl.BlockSpec((1, LEFT_ROWS, 2 * TILE_SIDE), lambda section: (section, 0, 0)),
            pl.BlockSpec((2, RIGHT_ROWS, 2 * TILE_SIDE), lambda section: (section, 0, 0)),
        ],
        out_specs=pl.BlockSpec((SINK_SLOTS * TILE_SIDE // 2, 2 * TILE_SIDE), lambda section: (0, 0)),
        scratch_shapes=[
            pltpu.VMEM((LEFT_SLOTS * RIGHT_SLOTS // 2, TILE_SIDE, 2 * TILE_SIDE), jnp.float32),
            pltpu.VMEM((2 * SINK_SLOTS, TILE_SIDE, 2 * TILE_SIDE), jnp.float32),
        ],
        name="product_sums",
    )(left_lists, right_lists, sink_lists, counts, left_all, right_all)


def per_device(rows, cols, left_blocks, right_blocks, left_slots, right_slots, sink_slots, live_counts):
    right = right_blocks.reshape(RIGHT_ROWS, 2 * TILE_SIDE)
    left = left_blocks.reshape(2, LEFT_SLOTS, TILE_SIDE // 2, 2 * TILE_SIDE).transpose(0, 2, 1, 3).reshape(LEFT_ROWS, 2 * TILE_SIDE)
    left_all, right_all = exchange(rows, cols, left, right)
    total = product_sums(
        left_slots.reshape(PANELS, PRODUCTS), right_slots.reshape(PANELS, PRODUCTS),
        sink_slots.reshape(PANELS, PRODUCTS), live_counts.reshape(PANELS), left_all, right_all)
    return total.reshape(1, 1, SINK_SLOTS, TILE_SIDE * TILE_SIDE)


def solution(mesh):
    return jax.shard_map(
        functools.partial(per_device, mesh.shape["row"], mesh.shape["col"]),
        mesh=mesh,
        in_specs=(
            P("row", "col", None, None),
            P("row", "col", None, None),
            P("row", "col", None, None, None),
            P("row", "col", None, None, None),
            P("row", "col", None, None, None),
            P("row", "col", None, None),
        ),
        out_specs=P("row", "col", None, None),
        check_vma=False,
    )
```

```python
import functools

import jax
import jax.numpy as jnp
from jax import lax
from jax.experimental import pallas as pl
from jax.experimental.pallas import tpu as pltpu
from jax.sharding import PartitionSpec as P

TILE_SIDE = 64
LEFT_SLOTS = 4
RIGHT_SLOTS = 20
SINK_SLOTS = 12
PRODUCTS = 24
SECTIONS = 4
PANELS = 2 * SECTIONS
CHUNKS = 4
LEFT_ROWS = LEFT_SLOTS * TILE_SIDE
RIGHT_ROWS = RIGHT_SLOTS * TILE_SIDE // 2
CHUNK_ROWS = RIGHT_ROWS // CHUNKS
TURNED = 3 * CHUNKS // 4
MESH = pl.DeviceIdType.MESH


def chosen(column, values):
    total = 0
    for place, value in enumerate(values):
        if value:
            total = total + (column % len(values) == place).astype(jnp.int32) * value
    return total


def exchange_kernel(rows, cols, left_ref, right_ref, left_all, right_all, relay,
                    left_send, left_recv, entry_send, right_recv, down_send, up_send,
                    relay_send, relay_recv):
    row = lax.axis_index("row")
    column = lax.axis_index("col")
    parity = row % 2
    half_row = row // 2
    below = (row + rows - 1) % rows
    above = (row + 1) % rows
    offset = chosen(column, (0, 0, 0, 6, 6, 6, 4, 2))
    turned_offset = chosen(column, (0, 6, 0, 6, 0, 6, 4, 2))
    relay_shift = chosen(column, (0, rows - 4, 0, 0, 4, 0, 0, 0))
    relays = relay_shift != 0
    shift = (2 * column + offset) % rows
    final_shift = (2 * column + turned_offset + rows - relay_shift) % rows
    moves = shift != 0
    greets_final = relays & (final_shift != relay_shift)

    def greet(row_to, column_to):
        pl.semaphore_signal(barrier, inc=1, device_id=(row_to, column_to), device_id_type=MESH)

    barrier = pltpu.get_barrier_semaphore()
    greet(below, column)
    greet(above, column)

    @pl.when(moves)
    def _():
        greet((row + shift) % rows, column)

    @pl.when(relays)
    def _():
        greet((row + relay_shift) % rows, column)

    @pl.when(greets_final)
    def _():
        greet((row + final_shift) % rows, column)

    for section in range(SECTIONS):
        @pl.when((half_row + section) % cols != 0)
        def _():
            greet(row, (column + half_row + section) % cols)

    peers = 2 + moves.astype(jnp.int32) + relays.astype(jnp.int32) + greets_final.astype(jnp.int32)
    for section in range(SECTIONS):
        peers += ((half_row + section) % cols != 0).astype(jnp.int32)
    pl.semaphore_wait(barrier, peers)

    def entry_of(chunk):
        if isinstance(chunk, int):
            return parity + (turned_offset if chunk < TURNED else offset)
        return parity + offset + (chunk < TURNED).astype(jnp.int32) * (turned_offset - offset)

    def part(chunk):
        return pl.ds(pl.multiple_of(chunk * CHUNK_ROWS, 8), CHUNK_ROWS)

    def entry_copy(chunk):
        return pltpu.make_async_remote_copy(
            src_ref=right_ref.at[part(chunk)], dst_ref=right_all.at[entry_of(chunk), part(chunk)],
            send_sem=entry_send.at[chunk], recv_sem=right_recv.at[entry_of(chunk), chunk],
            device_id=((row + rows - shift) % rows, column), device_id_type=MESH)

    def local_copy(chunk):
        return pltpu.make_async_copy(
            right_ref.at[part(chunk)], right_all.at[entry_of(chunk), part(chunk)],
            right_recv.at[entry_of(chunk), chunk])

    def relay_copy(chunk):
        return pltpu.make_async_remote_copy(
            src_ref=right_ref.at[part(chunk)], dst_ref=relay.at[part(chunk)],
            send_sem=entry_send.at[chunk], recv_sem=relay_recv.at[chunk],
            device_id=((row + rows - relay_shift) % rows, column), device_id_type=MESH)

    def final_copy(chunk):
        return pltpu.make_async_remote_copy(
            src_ref=relay.at[part(chunk)], dst_ref=right_all.at[entry_of(chunk), part(chunk)],
            send_sem=relay_send.at[chunk], recv_sem=right_recv.at[entry_of(chunk), chunk],
            device_id=((row + rows - final_shift) % rows, column), device_id_type=MESH)

    def left_copy(section):
        target = (column + 2 * cols - half_row - section) % cols
        return pltpu.make_async_remote_copy(
            src_ref=left_ref, dst_ref=left_all.at[section],
            send_sem=left_send.at[section], recv_sem=left_recv.at[section],
            device_id=(row, target), device_id_type=MESH)

    def left_local(section):
        return pltpu.make_async_copy(left_ref, left_all.at[section], left_recv.at[section])

    def down_copy(slot, chunk):
        return pltpu.make_async_remote_copy(
            src_ref=right_all.at[slot, part(chunk)],
            dst_ref=right_all.at[slot + 2 * (1 - parity), part(chunk)],
            send_sem=down_send.at[slot, chunk],
            recv_sem=right_recv.at[slot + 2 * (1 - parity), chunk],
            device_id=(below, column), device_id_type=MESH)

    def up_copy(slot, chunk):
        return pltpu.make_async_remote_copy(
            src_ref=right_all.at[slot, part(chunk)],
            dst_ref=right_all.at[slot - 2 * parity, part(chunk)],
            send_sem=up_send.at[slot, chunk],
            recv_sem=right_recv.at[slot - 2 * parity, chunk],
            device_id=(above, column), device_id_type=MESH)

    for chunk in range(CHUNKS):
        direct = moves if chunk >= TURNED else moves & jnp.logical_not(relays)

        @pl.when(direct)
        def _():
            entry_copy(chunk).start()

        @pl.when(jnp.logical_not(moves))
        def _():
            local_copy(chunk).start()

        if chunk < TURNED:
            @pl.when(relays)
            def _():
                relay_copy(chunk).start()

    for section in range(SECTIONS):
        @pl.when((half_row + section) % cols != 0)
        def _():
            left_copy(section).start()

        @pl.when((half_row + section) % cols == 0)
        def _():
            left_local(section).start()

    last_down = PANELS - 1 - 2 * (1 - parity)
    last_up = 2 * parity

    def arrived(slot, chunk):
        pltpu.make_async_copy(
            right_ref.at[part(chunk)], right_all.at[slot, part(chunk)], right_recv.at[slot, chunk]).wait()

    def first(chunk, carry):
        entry = entry_of(chunk)
        arrived(entry, chunk)

        @pl.when(entry <= last_down)
        def _():
            down_copy(entry, chunk).start()

        @pl.when(entry >= last_up)
        def _():
            up_copy(entry, chunk).start()
        return carry

    lax.fori_loop(TURNED, CHUNKS, first, 0)

    @pl.when(relays)
    def _():
        for chunk in range(TURNED):
            relay_copy(chunk).wait_recv()
            final_copy(chunk).start()

    lax.fori_loop(0, TURNED, first, 0)

    def onward(step, carry):
        distance = step // CHUNKS + 1
        chunk = (step + TURNED) % CHUNKS
        higher = entry_of(chunk) + distance
        lower = entry_of(chunk) - distance

        @pl.when(higher < PANELS)
        def _():
            arrived(higher, chunk)

        @pl.when(higher <= last_down)
        def _():
            down_copy(higher, chunk).start()

        @pl.when(lower >= 0)
        def _():
            arrived(lower, chunk)

        @pl.when(lower >= last_up)
        def _():
            up_copy(lower, chunk).start()
        return carry

    lax.fori_loop(0, (PANELS - 1) * CHUNKS, onward, 0)

    def sent(step, carry):
        slot = step // CHUNKS
        chunk = step % CHUNKS
        entry = entry_of(chunk)

        @pl.when((slot >= entry) & (slot <= last_down))
        def _():
            down_copy(slot, chunk).wait_send()

        @pl.when((slot <= entry) & (slot >= last_up))
        def _():
            up_copy(slot, chunk).wait_send()
        return carry

    lax.fori_loop(0, PANELS * CHUNKS, sent, 0)

    for chunk in range(CHUNKS):
        @pl.when(moves)
        def _():
            entry_copy(chunk).wait_send()

        if chunk < TURNED:
            @pl.when(relays)
            def _():
                final_copy(chunk).wait_send()

    for section in range(SECTIONS):
        @pl.when((half_row + section) % cols != 0)
        def _():
            left_copy(section).wait()

        @pl.when((half_row + section) % cols == 0)
        def _():
            left_local(section).wait()


def exchange(rows, cols, left, right):
    dma = pltpu.SemaphoreType.DMA
    return pl.pallas_call(
        functools.partial(exchange_kernel, rows, cols),
        out_shape=(
            jax.ShapeDtypeStruct((SECTIONS, LEFT_ROWS, 2 * TILE_SIDE), jnp.float32),
            jax.ShapeDtypeStruct((PANELS, RIGHT_ROWS, 2 * TILE_SIDE), jnp.float32),
        ),
        in_specs=[pl.BlockSpec(memory_space=pltpu.VMEM)] * 2,
        out_specs=(pl.BlockSpec(memory_space=pltpu.VMEM),) * 2,
        scratch_shapes=[
            pltpu.VMEM((TURNED * CHUNK_ROWS, 2 * TILE_SIDE), jnp.float32),
            dma((SECTIONS,)), dma((SECTIONS,)), dma((CHUNKS,)), dma((PANELS, CHUNKS)),
            dma((PANELS, CHUNKS)), dma((PANELS, CHUNKS)), dma((TURNED,)), dma((TURNED,)),
        ],
        compiler_params=pltpu.CompilerParams(collective_id=0, has_side_effects=True),
        name="exchange",
    )(left, right)


def product_kernel(left_lists, right_lists, sink_lists, counts, left_all, right_all, out, products, sums):
    side = TILE_SIDE
    section = pl.program_id(0)

    @pl.when(section == 0)
    def _():
        sums[...] = jnp.zeros_like(sums)

    def ordered(count):
        return lax.broadcasted_iota(jnp.int32, (count, 2 * side), 1) < side

    place = lax.broadcasted_iota(jnp.int32, (2 * side, 2 * side), 0)
    target = lax.broadcasted_iota(jnp.int32, (2 * side, 2 * side), 1)
    moved = (place & side) + (place & 1) * (side // 2) + ((place & (side - 1)) >> 1)
    evens_first = (moved == target).astype(jnp.float32).astype(jnp.bfloat16)
    rows = LEFT_ROWS // 2
    low_lanes, low_lanes_left = ordered(side // 2), ordered(rows)
    for half in range(2):
        left = jnp.concatenate(
            [left_all[0, pl.ds(half * rows + slot, side // 2, stride=LEFT_SLOTS), :] for slot in range(LEFT_SLOTS)],
            axis=0)
        turned = pltpu.roll(left, side, 1)
        even = jnp.where(low_lanes_left, left, turned).reshape(LEFT_SLOTS, side // 2, 2 * side)
        odd = jnp.where(low_lanes_left, turned, left).reshape(LEFT_SLOTS, side // 2, 2 * side)
        twice = jnp.concatenate([even, odd], axis=1).reshape(LEFT_ROWS, 2 * side)
        high = twice.astype(jnp.bfloat16).astype(jnp.float32)
        split = jnp.where(ordered(LEFT_ROWS), high, twice - high).astype(jnp.bfloat16)
        split = jnp.dot(split, evens_first, preferred_element_type=jnp.float32).astype(jnp.bfloat16)
        stream = jnp.concatenate([split, split], axis=1)
        item = 2 * section + half
        for quad in range(RIGHT_SLOTS // 4):
            pairs = []
            for pair in range(2):
                base = (4 * quad + 2 * pair) * (side // 2)
                first = right_all[half, pl.ds(base, side // 2), :]
                second = right_all[half, pl.ds(base + side // 2, side // 2), :]
                pairs.append(jnp.concatenate([
                    jnp.where(low_lanes, first, pltpu.roll(second, side, 1)),
                    jnp.where(low_lanes, pltpu.roll(first, side, 1), second)], axis=0))
            right = jnp.concatenate(pairs, axis=1)
            right_high = right.astype(jnp.bfloat16)
            right_low = (right - right_high.astype(jnp.float32)).astype(jnp.bfloat16)
            held = jnp.concatenate([right_high, right_high, right_low, right_low], axis=0)
            found = jnp.dot(stream, held, preferred_element_type=jnp.float32)
            for n in range(2):
                products[pl.ds(LEFT_SLOTS * (2 * quad + n), LEFT_SLOTS)] = (
                    found[:, 2 * side * n : 2 * side * (n + 1)].reshape(LEFT_SLOTS, side, 2 * side))

        def listed(position):
            right_slot = right_lists[item, position]
            source = LEFT_SLOTS * (right_slot >> 1) + left_lists[item, position]
            return source, 2 * sink_lists[item, position] + (right_slot & 1)

        def add(position, ahead):
            source, sink = ahead
            following = listed(jnp.minimum(position + 1, PRODUCTS - 1))
            sums[sink] += products[source]
            return following

        lax.fori_loop(0, counts[item], add, listed(0))

    @pl.when(section == SECTIONS - 1)
    def _():
        for sink in range(SINK_SLOTS):
            total = sums[2 * sink] + pltpu.roll(sums[2 * sink + 1], side, 1)
            out[pl.ds(sink * (side // 2), side // 2), :] = jnp.where(
                low_lanes, total[: side // 2], pltpu.roll(total[side // 2 :], side, 1))


def product_sums(left_lists, right_lists, sink_lists, counts, left_all, right_all):
    smem = pl.BlockSpec(memory_space=pltpu.SMEM)
    return pl.pallas_call(
        product_kernel,
        out_shape=jax.ShapeDtypeStruct((SINK_SLOTS * TILE_SIDE // 2, 2 * TILE_SIDE), jnp.float32),
        grid=(SECTIONS,),
        in_specs=[smem] * 4 + [
            pl.BlockSpec((1, LEFT_ROWS, 2 * TILE_SIDE), lambda section: (section, 0, 0)),
            pl.BlockSpec((2, RIGHT_ROWS, 2 * TILE_SIDE), lambda section: (section, 0, 0)),
        ],
        out_specs=pl.BlockSpec((SINK_SLOTS * TILE_SIDE // 2, 2 * TILE_SIDE), lambda section: (0, 0)),
        scratch_shapes=[
            pltpu.VMEM((LEFT_SLOTS * RIGHT_SLOTS // 2, TILE_SIDE, 2 * TILE_SIDE), jnp.float32),
            pltpu.VMEM((2 * SINK_SLOTS, TILE_SIDE, 2 * TILE_SIDE), jnp.float32),
        ],
        name="product_sums",
    )(left_lists, right_lists, sink_lists, counts, left_all, right_all)


def per_device(rows, cols, left_blocks, right_blocks, left_slots, right_slots, sink_slots, live_counts):
    right = right_blocks.reshape(RIGHT_ROWS, 2 * TILE_SIDE)
    left = left_blocks.reshape(2, LEFT_SLOTS, TILE_SIDE // 2, 2 * TILE_SIDE).transpose(0, 2, 1, 3).reshape(LEFT_ROWS, 2 * TILE_SIDE)
    left_all, right_all = exchange(rows, cols, left, right)
    total = product_sums(
        left_slots.reshape(PANELS, PRODUCTS), right_slots.reshape(PANELS, PRODUCTS),
        sink_slots.reshape(PANELS, PRODUCTS), live_counts.reshape(PANELS), left_all, right_all)
    return total.reshape(1, 1, SINK_SLOTS, TILE_SIDE * TILE_SIDE)


def solution(mesh):
    return jax.shard_map(
        functools.partial(per_device, mesh.shape["row"], mesh.shape["col"]),
        mesh=mesh,
        in_specs=(
            P("row", "col", None, None),
            P("row", "col", None, None),
            P("row", "col", None, None, None),
            P("row", "col", None, None, None),
            P("row", "col", None, None, None),
            P("row", "col", None, None),
        ),
        out_specs=P("row", "col", None, None),
        check_vma=False,
    )
```

```python
import functools

import jax
import jax.numpy as jnp
from jax import lax
from jax.experimental import pallas as pl
from jax.experimental.pallas import tpu as pltpu
from jax.sharding import PartitionSpec as P

TILE_SIDE = 64
LEFT_SLOTS = 4
RIGHT_SLOTS = 20
SINK_SLOTS = 12
PRODUCTS = 24
SECTIONS = 4
PANELS = 2 * SECTIONS
CHUNKS = 2
LEFT_ROWS = LEFT_SLOTS * TILE_SIDE
RIGHT_ROWS = RIGHT_SLOTS * TILE_SIDE // 2
CHUNK_ROWS = RIGHT_ROWS // CHUNKS
TURNED = CHUNKS // 2
MESH = pl.DeviceIdType.MESH


def chosen(column, values):
    total = 0
    for place, value in enumerate(values):
        if value:
            total = total + (column % len(values) == place).astype(jnp.int32) * value
    return total


def exchange_kernel(rows, cols, left_ref, right_ref, left_all, right_all, relay,
                    left_send, left_recv, entry_send, right_recv, down_send, up_send,
                    relay_send, relay_recv):
    row = lax.axis_index("row")
    column = lax.axis_index("col")
    parity = row % 2
    half_row = row // 2
    below = (row + rows - 1) % rows
    above = (row + 1) % rows
    offset = chosen(column, (0, 0, 0, 6, 6, 6, 4, 2))
    turned_offset = chosen(column, (0, 6, 0, 6, 0, 6, 4, 2))
    relay_shift = chosen(column, (0, rows - 4, 0, 0, 4, 0, 0, 0))
    relays = relay_shift != 0
    shift = (2 * column + offset) % rows
    final_shift = (2 * column + turned_offset + rows - relay_shift) % rows
    moves = shift != 0
    greets_final = relays & (final_shift != relay_shift)

    def greet(row_to, column_to):
        pl.semaphore_signal(barrier, inc=1, device_id=(row_to, column_to), device_id_type=MESH)

    barrier = pltpu.get_barrier_semaphore()
    greet(below, column)
    greet(above, column)

    @pl.when(moves)
    def _():
        greet((row + shift) % rows, column)

    @pl.when(relays)
    def _():
        greet((row + relay_shift) % rows, column)

    @pl.when(greets_final)
    def _():
        greet((row + final_shift) % rows, column)

    for section in range(SECTIONS):
        @pl.when((half_row + section) % cols != 0)
        def _():
            greet(row, (column + half_row + section) % cols)

    peers = 2 + moves.astype(jnp.int32) + relays.astype(jnp.int32) + greets_final.astype(jnp.int32)
    for section in range(SECTIONS):
        peers += ((half_row + section) % cols != 0).astype(jnp.int32)
    pl.semaphore_wait(barrier, peers)

    def entry_of(chunk):
        if isinstance(chunk, int):
            return parity + (turned_offset if chunk < TURNED else offset)
        return parity + offset + (chunk < TURNED).astype(jnp.int32) * (turned_offset - offset)

    def part(chunk):
        return pl.ds(pl.multiple_of(chunk * CHUNK_ROWS, 8), CHUNK_ROWS)

    def entry_copy(chunk):
        return pltpu.make_async_remote_copy(
            src_ref=right_ref.at[part(chunk)], dst_ref=right_all.at[entry_of(chunk), part(chunk)],
            send_sem=entry_send.at[chunk], recv_sem=right_recv.at[entry_of(chunk), chunk],
            device_id=((row + rows - shift) % rows, column), device_id_type=MESH)

    def local_copy(chunk):
        return pltpu.make_async_copy(
            right_ref.at[part(chunk)], right_all.at[entry_of(chunk), part(chunk)],
            right_recv.at[entry_of(chunk), chunk])

    def relay_copy(chunk):
        return pltpu.make_async_remote_copy(
            src_ref=right_ref.at[part(chunk)], dst_ref=relay.at[part(chunk)],
            send_sem=entry_send.at[chunk], recv_sem=relay_recv.at[chunk],
            device_id=((row + rows - relay_shift) % rows, column), device_id_type=MESH)

    def final_copy(chunk):
        return pltpu.make_async_remote_copy(
            src_ref=relay.at[part(chunk)], dst_ref=right_all.at[entry_of(chunk), part(chunk)],
            send_sem=relay_send.at[chunk], recv_sem=right_recv.at[entry_of(chunk), chunk],
            device_id=((row + rows - final_shift) % rows, column), device_id_type=MESH)

    def left_copy(section):
        target = (column + 2 * cols - half_row - section) % cols
        return pltpu.make_async_remote_copy(
            src_ref=left_ref, dst_ref=left_all.at[section],
            send_sem=left_send.at[section], recv_sem=left_recv.at[section],
            device_id=(row, target), device_id_type=MESH)

    def left_local(section):
        return pltpu.make_async_copy(left_ref, left_all.at[section], left_recv.at[section])

    def down_copy(slot, chunk):
        return pltpu.make_async_remote_copy(
            src_ref=right_all.at[slot, part(chunk)],
            dst_ref=right_all.at[slot + 2 * (1 - parity), part(chunk)],
            send_sem=down_send.at[slot, chunk],
            recv_sem=right_recv.at[slot + 2 * (1 - parity), chunk],
            device_id=(below, column), device_id_type=MESH)

    def up_copy(slot, chunk):
        return pltpu.make_async_remote_copy(
            src_ref=right_all.at[slot, part(chunk)],
            dst_ref=right_all.at[slot - 2 * parity, part(chunk)],
            send_sem=up_send.at[slot, chunk],
            recv_sem=right_recv.at[slot - 2 * parity, chunk],
            device_id=(above, column), device_id_type=MESH)

    for chunk in range(CHUNKS):
        direct = moves if chunk >= TURNED else moves & jnp.logical_not(relays)

        @pl.when(direct)
        def _():
            entry_copy(chunk).start()

        @pl.when(jnp.logical_not(moves))
        def _():
            local_copy(chunk).start()

        if chunk < TURNED:
            @pl.when(relays)
            def _():
                relay_copy(chunk).start()

    for section in range(SECTIONS):
        @pl.when((half_row + section) % cols != 0)
        def _():
            left_copy(section).start()

        @pl.when((half_row + section) % cols == 0)
        def _():
            left_local(section).start()

    last_down = PANELS - 1 - 2 * (1 - parity)
    last_up = 2 * parity

    def arrived(slot, chunk):
        pltpu.make_async_copy(
            right_ref.at[part(chunk)], right_all.at[slot, part(chunk)], right_recv.at[slot, chunk]).wait()

    def first(chunk, carry):
        entry = entry_of(chunk)
        arrived(entry, chunk)

        @pl.when(entry <= last_down)
        def _():
            down_copy(entry, chunk).start()

        @pl.when(entry >= last_up)
        def _():
            up_copy(entry, chunk).start()
        return carry

    lax.fori_loop(TURNED, CHUNKS, first, 0)

    @pl.when(relays)
    def _():
        for chunk in range(TURNED):
            relay_copy(chunk).wait_recv()
            final_copy(chunk).start()

    lax.fori_loop(0, TURNED, first, 0)

    def onward(step, carry):
        distance = step // CHUNKS + 1
        chunk = (step + TURNED) % CHUNKS
        higher = entry_of(chunk) + distance
        lower = entry_of(chunk) - distance

        @pl.when(higher < PANELS)
        def _():
            arrived(higher, chunk)

        @pl.when(higher <= last_down)
        def _():
            down_copy(higher, chunk).start()

        @pl.when(lower >= 0)
        def _():
            arrived(lower, chunk)

        @pl.when(lower >= last_up)
        def _():
            up_copy(lower, chunk).start()
        return carry

    lax.fori_loop(0, (PANELS - 1) * CHUNKS, onward, 0)

    def sent(step, carry):
        slot = step // CHUNKS
        chunk = step % CHUNKS
        entry = entry_of(chunk)

        @pl.when((slot >= entry) & (slot <= last_down))
        def _():
            down_copy(slot, chunk).wait_send()

        @pl.when((slot <= entry) & (slot >= last_up))
        def _():
            up_copy(slot, chunk).wait_send()
        return carry

    lax.fori_loop(0, PANELS * CHUNKS, sent, 0)

    for chunk in range(CHUNKS):
        @pl.when(moves)
        def _():
            entry_copy(chunk).wait_send()

        if chunk < TURNED:
            @pl.when(relays)
            def _():
                final_copy(chunk).wait_send()

    for section in range(SECTIONS):
        @pl.when((half_row + section) % cols != 0)
        def _():
            left_copy(section).wait()

        @pl.when((half_row + section) % cols == 0)
        def _():
            left_local(section).wait()


def exchange(rows, cols, left, right):
    dma = pltpu.SemaphoreType.DMA
    return pl.pallas_call(
        functools.partial(exchange_kernel, rows, cols),
        out_shape=(
            jax.ShapeDtypeStruct((SECTIONS, LEFT_ROWS, 2 * TILE_SIDE), jnp.float32),
            jax.ShapeDtypeStruct((PANELS, RIGHT_ROWS, 2 * TILE_SIDE), jnp.float32),
        ),
        in_specs=[pl.BlockSpec(memory_space=pltpu.VMEM)] * 2,
        out_specs=(pl.BlockSpec(memory_space=pltpu.VMEM),) * 2,
        scratch_shapes=[
            pltpu.VMEM((TURNED * CHUNK_ROWS, 2 * TILE_SIDE), jnp.float32),
            dma((SECTIONS,)), dma((SECTIONS,)), dma((CHUNKS,)), dma((PANELS, CHUNKS)),
            dma((PANELS, CHUNKS)), dma((PANELS, CHUNKS)), dma((TURNED,)), dma((TURNED,)),
        ],
        compiler_params=pltpu.CompilerParams(collective_id=0, has_side_effects=True),
        name="exchange",
    )(left, right)


def product_kernel(left_lists, right_lists, sink_lists, counts, left_all, right_all, out, products, sums):
    side = TILE_SIDE
    section = pl.program_id(0)

    @pl.when(section == 0)
    def _():
        sums[...] = jnp.zeros_like(sums)

    def ordered(count):
        return lax.broadcasted_iota(jnp.int32, (count, 2 * side), 1) < side

    place = lax.broadcasted_iota(jnp.int32, (2 * side, 2 * side), 0)
    target = lax.broadcasted_iota(jnp.int32, (2 * side, 2 * side), 1)
    moved = (place & side) + (place & 1) * (side // 2) + ((place & (side - 1)) >> 1)
    evens_first = (moved == target).astype(jnp.float32).astype(jnp.bfloat16)
    rows = LEFT_ROWS // 2
    low_lanes, low_lanes_left = ordered(side // 2), ordered(rows)
    for half in range(2):
        left = jnp.concatenate(
            [left_all[0, pl.ds(half * rows + slot, side // 2, stride=LEFT_SLOTS), :] for slot in range(LEFT_SLOTS)],
            axis=0)
        turned = pltpu.roll(left, side, 1)
        even = jnp.where(low_lanes_left, left, turned).reshape(LEFT_SLOTS, side // 2, 2 * side)
        odd = jnp.where(low_lanes_left, turned, left).reshape(LEFT_SLOTS, side // 2, 2 * side)
        twice = jnp.concatenate([even, odd], axis=1).reshape(LEFT_ROWS, 2 * side)
        high = twice.astype(jnp.bfloat16).astype(jnp.float32)
        split = jnp.where(ordered(LEFT_ROWS), high, twice - high).astype(jnp.bfloat16)
        split = jnp.dot(split, evens_first, preferred_element_type=jnp.float32).astype(jnp.bfloat16)
        stream = jnp.concatenate([split, split], axis=1)
        item = 2 * section + half
        for quad in range(RIGHT_SLOTS // 4):
            pairs = []
            for pair in range(2):
                base = (4 * quad + 2 * pair) * (side // 2)
                first = right_all[half, pl.ds(base, side // 2), :]
                second = right_all[half, pl.ds(base + side // 2, side // 2), :]
                pairs.append(jnp.concatenate([
                    jnp.where(low_lanes, first, pltpu.roll(second, side, 1)),
                    jnp.where(low_lanes, pltpu.roll(first, side, 1), second)], axis=0))
            right = jnp.concatenate(pairs, axis=1)
            right_high = right.astype(jnp.bfloat16)
            right_low = (right - right_high.astype(jnp.float32)).astype(jnp.bfloat16)
            held = jnp.concatenate([right_high, right_high, right_low, right_low], axis=0)
            found = jnp.dot(stream, held, preferred_element_type=jnp.float32)
            for n in range(2):
                products[pl.ds(LEFT_SLOTS * (2 * quad + n), LEFT_SLOTS)] = (
                    found[:, 2 * side * n : 2 * side * (n + 1)].reshape(LEFT_SLOTS, side, 2 * side))

        def listed(position):
            right_slot = right_lists[item, position]
            source = LEFT_SLOTS * (right_slot >> 1) + left_lists[item, position]
            return source, 2 * sink_lists[item, position] + (right_slot & 1)

        def add(position, ahead):
            source, sink = ahead
            following = listed(jnp.minimum(position + 1, PRODUCTS - 1))
            sums[sink] += products[source]
            return following

        lax.fori_loop(0, counts[item], add, listed(0))

    @pl.when(section == SECTIONS - 1)
    def _():
        for sink in range(SINK_SLOTS):
            total = sums[2 * sink] + pltpu.roll(sums[2 * sink + 1], side, 1)
            out[pl.ds(sink * (side // 2), side // 2), :] = jnp.where(
                low_lanes, total[: side // 2], pltpu.roll(total[side // 2 :], side, 1))


def product_sums(left_lists, right_lists, sink_lists, counts, left_all, right_all):
    smem = pl.BlockSpec(memory_space=pltpu.SMEM)
    return pl.pallas_call(
        product_kernel,
        out_shape=jax.ShapeDtypeStruct((SINK_SLOTS * TILE_SIDE // 2, 2 * TILE_SIDE), jnp.float32),
        grid=(SECTIONS,),
        in_specs=[smem] * 4 + [
            pl.BlockSpec((1, LEFT_ROWS, 2 * TILE_SIDE), lambda section: (section, 0, 0)),
            pl.BlockSpec((2, RIGHT_ROWS, 2 * TILE_SIDE), lambda section: (section, 0, 0)),
        ],
        out_specs=pl.BlockSpec((SINK_SLOTS * TILE_SIDE // 2, 2 * TILE_SIDE), lambda section: (0, 0)),
        scratch_shapes=[
            pltpu.VMEM((LEFT_SLOTS * RIGHT_SLOTS // 2, TILE_SIDE, 2 * TILE_SIDE), jnp.float32),
            pltpu.VMEM((2 * SINK_SLOTS, TILE_SIDE, 2 * TILE_SIDE), jnp.float32),
        ],
        name="product_sums",
    )(left_lists, right_lists, sink_lists, counts, left_all, right_all)


def per_device(rows, cols, left_blocks, right_blocks, left_slots, right_slots, sink_slots, live_counts):
    right = right_blocks.reshape(RIGHT_ROWS, 2 * TILE_SIDE)
    left = left_blocks.reshape(2, LEFT_SLOTS, TILE_SIDE // 2, 2 * TILE_SIDE).transpose(0, 2, 1, 3).reshape(LEFT_ROWS, 2 * TILE_SIDE)
    left_all, right_all = exchange(rows, cols, left, right)
    total = product_sums(
        left_slots.reshape(PANELS, PRODUCTS), right_slots.reshape(PANELS, PRODUCTS),
        sink_slots.reshape(PANELS, PRODUCTS), live_counts.reshape(PANELS), left_all, right_all)
    return total.reshape(1, 1, SINK_SLOTS, TILE_SIDE * TILE_SIDE)


def solution(mesh):
    return jax.shard_map(
        functools.partial(per_device, mesh.shape["row"], mesh.shape["col"]),
        mesh=mesh,
        in_specs=(
            P("row", "col", None, None),
            P("row", "col", None, None),
            P("row", "col", None, None, None),
            P("row", "col", None, None, None),
            P("row", "col", None, None, None),
            P("row", "col", None, None),
        ),
        out_specs=P("row", "col", None, None),
        check_vma=False,
    )
```
